256 devices in a mesh: seq: 32 (over z, y), head: 8 (over x, core).
Axes of the slice: x: 4, y: 4, z: 8, core: 2. Of those that a mesh axis runs over, the one named last changes fastest.
Arguments:
- queries: bfloat16 [1, 32768, 4096], P(None, ('seq', 'head')), may hold values from -4 to 4
- keys: bfloat16 [1, 32768, 4096], P(None, ('seq', 'head')), may hold values from -4 to 4
- values: bfloat16 [1, 32768, 4096], P(None, ('seq', 'head')), may hold values from -6 to 6
- features: bfloat16 [32, 256, 128], P('head'), may hold values from -4 to 4
Outputs:
- attended: bfloat16 [1, 32768, 4096], P(None, ('seq', 'head'))
The draws below stay inside these ranges and needn't reach their ends.
All inputs are finite; a program needn't handle non-finite values.
Results may differ from the reference program's by a relative error of at most 0.0065.
Values may be sent and summed in bfloat16 or wider, within the bound.
A program may use at most 128 MiB of HBM per device.

```python
import math
import jax
import jax.numpy as jnp
from jax import lax

H = 32
DH = 128
M = 256
SEG = 1024
BATCH = 1
WIDTH = 4096
LENGTH = 32768


def shard_levels(key, dims, cuts, low, top_value):
    level, own = 1.0, jax.random.fold_in(key, 6)
    for axis_at, blocks in cuts:
        steps = jnp.exp(jax.random.uniform(jax.random.fold_in(own, axis_at), (blocks,), jnp.float32, low / len(cuts), top_value / len(cuts)))
        level = level * jnp.repeat(steps, dims[axis_at] // blocks).reshape([-1 if axis == axis_at else 1 for axis in range(len(dims))])
    return level


def gaussian(key, dims, width, reach, pieces=(), held_as=jnp.bfloat16):
    factor_of = shard_levels(key, dims, pieces, -0.22, 0.18) if pieces else 1.0
    values = jax.random.normal(key, dims, jnp.float32) * width * factor_of
    return jnp.minimum(jnp.maximum(values, -reach), reach).astype(held_as)


def setup_inputs(seed: int = 0) -> dict:
    streams_of = jax.random.split(jax.random.key(seed), 5)
    return {
        "queries": gaussian(streams_of[0], (BATCH, LENGTH, WIDTH), 1.0, 4.0, ((1, 256),)),
        "keys": gaussian(streams_of[1], (BATCH, LENGTH, WIDTH), 1.0, 4.0, ((1, 256),)),
        "values": gaussian(streams_of[2], (BATCH, LENGTH, WIDTH), 1.0, 6.0, ((1, 256),)),
        "features": gaussian(streams_of[3], (H, M, DH), 1.0, 4.0, ((0, 8),)),
    }


def feature_map(source, projection_directions):
    root_scale = DH ** (-0.25)
    widened = source.astype(jnp.float32)
    square_sum = lax.optimization_barrier(jnp.sum(widened * widened, axis=-1, keepdims=True))
    row_factor = lax.rsqrt(square_sum / DH + 1e-06)
    wide_dirs = projection_directions.astype(jnp.float32)
    dir_factor = lax.rsqrt(lax.optimization_barrier(jnp.mean(wide_dirs * wide_dirs, axis=-1)) + 1e-06)
    projected = jnp.dot(source, projection_directions.T, preferred_element_type=jnp.float32)
    projected = projected * row_factor * dir_factor[None, :] * root_scale
    halved = 0.5 * root_scale * root_scale * square_sum * row_factor * row_factor
    return (jnp.exp(projected - halved) * (1.0 / math.sqrt(M))).astype(jnp.bfloat16)

def reference(queries, keys, values, features):
    blocks = LENGTH // SEG
    causal_mask = jnp.tril(jnp.ones((SEG, SEG), dtype=bool))

    def one_pair(index):
        batch_index = index // H
        head_index = index % H
        start = (head_index * DH).astype(jnp.int32)
        head_query_rows = lax.dynamic_slice_in_dim(queries[batch_index], start, DH, 1)
        key_head = lax.dynamic_slice_in_dim(keys[batch_index], start, DH, 1)
        value_head = lax.dynamic_slice_in_dim(values[batch_index], start, DH, 1)
        projection_directions = features[head_index]
        phi_q = feature_map(head_query_rows, projection_directions).reshape(blocks, SEG, M)
        phi_k = feature_map(key_head, projection_directions).reshape(blocks, SEG, M)
        value_blocks = value_head.reshape(blocks, SEG, DH)

        def advance(carried, block_contents):
            states, totals = carried
            block_q, block_k, block_v = block_contents
            scores = jnp.dot(block_q, block_k.T, preferred_element_type=jnp.float32)
            scores = jnp.where(causal_mask, scores, jnp.float32(0.0))
            widened_query = block_q.astype(jnp.float32)
            denominator = lax.optimization_barrier(jnp.sum(scores, axis=1)) + jnp.dot(widened_query, totals, precision=lax.Precision.HIGHEST)
            weights = scores.astype(jnp.bfloat16)
            numerator_sum = jnp.dot(weights, block_v, preferred_element_type=jnp.float32)
            numerator_sum = numerator_sum + jnp.dot(widened_query, states, precision=lax.Precision.HIGHEST)
            result = (numerator_sum / denominator[:, None]).astype(jnp.bfloat16)
            states = states + jnp.dot(block_k.T, block_v, preferred_element_type=jnp.float32)
            totals = totals + lax.optimization_barrier(jnp.sum(block_k.astype(jnp.float32), axis=0))
            return ((states, totals), result)
        start_state = (jnp.zeros((M, DH), jnp.float32), jnp.zeros((M,), jnp.float32))
        unused, result_list = lax.scan(advance, start_state, (phi_q, phi_k, value_blocks))
        return result_list.reshape(LENGTH, DH)
    outputs = lax.map(one_pair, jnp.arange(BATCH * H, dtype=jnp.int32))
    outputs = outputs.reshape(BATCH, H, LENGTH, DH)
    return jnp.transpose(outputs, (0, 2, 1, 3)).reshape(BATCH, LENGTH, H * DH)
```

```python
import math

import jax
import jax.numpy as jnp
from jax import lax
from jax.experimental import pallas as pl
from jax.experimental.pallas import tpu as pltpu
from jax.sharding import PartitionSpec as P

MESH = pl.DeviceIdType.MESH
NZ, NY, NX = 8, 4, 4
PLANE = NY * NX
WAVES = 4
EARLY = 2
LOG2E = 1.4426950408889634
F32 = jnp.float32
BF16 = jnp.bfloat16


def dot(a, b, contract):
    return lax.dot_general(a, b, ((contract[:1], contract[1:]), ((), ())), preferred_element_type=F32)


def kernel(
    q_hbm, k_hbm, v_hbm, w_hbm, out_hbm,
    qb, kb, vb, wb, scale, phi_q, num, den, ob,
    s_send, s_recv, t_send, t_recv, z_send, z_recv, zt_send, zt_recv,
    p_send, p_recv, pt_send, pt_recv,
    in_sem, ex_send, ex_recv, w_send, w_recv, wf_send, sc_send, sc_recv,
    s_ssem, s_rsem, t_ssem, t_rsem, z_ssem, z_rsem, zt_ssem, zt_rsem,
    p_ssem, p_rsem, pt_ssem, pt_rsem, o_sem, o_ssem, o_rsem,
):
    heads, tokens, head_size = num.shape
    feats = wb.shape[1]
    rows = tokens // 2
    per = heads // NX
    width = per * head_size
    part = feats // WAVES
    root = head_size ** (-0.25)

    seq = lax.axis_index("seq")
    pos = lax.axis_index("head")
    z, y = seq // NY, lax.rem(seq, NY)
    x, c = pos // 2, lax.rem(pos, 2)
    p_me = y * NX + x
    g_me = x * per + y
    other = 1 - c

    def dev(zz, yy, xx, cc):
        return (zz * NY + yy, xx * 2 + cc)

    def step(a, d, n):
        return lax.rem(a + d, n)

    def turned(k):
        return step(y, k // NX, NY), step(x, lax.rem(k, NX), NX)

    partner = dev(z, y, x, other)

    barrier = pltpu.get_barrier_semaphore()
    pl.semaphore_signal(barrier, inc=1, device_id=partner, device_id_type=MESH)

    @pl.loop(1, NZ)
    def _(d):
        pl.semaphore_signal(barrier, inc=1, device_id=dev(step(z, d, NZ), y, x, c), device_id_type=MESH)

    @pl.loop(1, PLANE)
    def _(k):
        yy, xx = turned(k)
        pl.semaphore_signal(barrier, inc=1, device_id=dev(z, yy, xx, c), device_id_type=MESH)

    def columns(slab, core):
        return pl.ds(pl.multiple_of((slab * 2 + core) * width, width), width)

    def mine(slab):
        return pl.ds(slab * width, width)

    my_rows = pl.ds(pl.multiple_of(c * rows, rows), rows)
    other_rows = pl.ds(pl.multiple_of(other * rows, rows), rows)

    w_local = pltpu.make_async_copy(w_hbm, wb.at[pl.ds(x * per, per)], in_sem.at[3])
    w_local.start()
    pairs = ((k_hbm, kb), (v_hbm, vb), (q_hbm, qb))
    for t, (src, dst) in enumerate(pairs):
        for slab in range(NX):
            pltpu.make_async_copy(src.at[:, columns(slab, c)], dst.at[my_rows, mine(slab)], in_sem.at[t]).start()

    w_local.wait()
    ones = jnp.ones((8, head_size), BF16)

    @pl.loop(0, per)
    def _(i):
        wide = wb[x * per + i].astype(F32)
        square = wide * wide
        high = square.astype(BF16)
        low = (square - high.astype(F32)).astype(BF16)
        total = dot(ones, high, (1, 1)) + dot(ones, low, (1, 1))
        scale[x * per + i] = lax.rsqrt(total[0:1] * (1.0 / head_size) + 1e-06)

    for t, (src, dst) in enumerate(pairs):
        pltpu.make_async_copy(dst.at[my_rows], dst.at[my_rows], in_sem.at[t]).wait()

    pl.semaphore_wait(barrier, NZ - 1 + PLANE)

    right, left, far = step(x, 1, NX), step(x, NX - 1, NX), step(x, 2, NX)

    def feature_copy(src, slab, i, target, sem):
        g = slab * per + i
        return pltpu.make_async_remote_copy(
            src_ref=src, dst_ref=wb.at[g], send_sem=sem, recv_sem=w_recv.at[g],
            device_id=dev(z, y, target, c), device_id_type=MESH,
        )

    for n in range(per):
        for direction, (target, i) in enumerate(((left, n), (right, (n + per // 2) % per))):
            feature_copy(w_hbm.at[i], x, i, target, w_send.at[direction, i]).start()

    def exchange(t):
        src, dst = pairs[t]
        for slab in range(NX):
            pltpu.make_async_remote_copy(
                src_ref=src.at[:, columns(slab, other)], dst_ref=dst.at[my_rows, mine(slab)],
                send_sem=ex_send.at[t], recv_sem=ex_recv.at[t], device_id=partner, device_id_type=MESH,
            ).start()

    def exchanged(t):
        dst = pairs[t][1]
        return pltpu.make_async_remote_copy(
            src_ref=dst.at[other_rows], dst_ref=dst.at[other_rows],
            send_sem=ex_send.at[t], recv_sem=ex_recv.at[t], device_id=partner, device_id_type=MESH,
        )

    def scale_copy(slab, target, sem):
        view = scale.at[pl.ds(slab * per, per)]
        return pltpu.make_async_remote_copy(
            src_ref=view, dst_ref=view, send_sem=sem, recv_sem=sc_recv.at[slab],
            device_id=dev(z, y, target, c), device_id_type=MESH,
        )

    for t in range(3):
        exchange(t)
    for n, target in enumerate((left, right, far)):
        scale_copy(x, target, sc_send.at[n]).start()
    for t in range(3):
        exchanged(t).wait_recv()

    def owner(g):
        return dev(z, lax.rem(g, per), g // per, c)

    def s_copy(g, w):
        view = pl.ds(w * part, part)
        return pltpu.make_async_remote_copy(
            src_ref=s_send.at[g, view], dst_ref=s_recv.at[p_me, view], send_sem=s_ssem,
            recv_sem=s_rsem.at[w, p_me], device_id=owner(g), device_id_type=MESH,
        )

    def t_copy(g):
        return pltpu.make_async_remote_copy(
            src_ref=t_send.at[g], dst_ref=t_recv.at[p_me], send_sem=t_ssem,
            recv_sem=t_rsem.at[p_me], device_id=owner(g), device_id_type=MESH,
        )

    at = lax.broadcasted_iota(jnp.int32, (tokens, tokens), 0)
    of = lax.broadcasted_iota(jnp.int32, (tokens, tokens), 1)
    causal = at >= of

    def mapped(source, dirs, dir_scale):
        wide = source.astype(F32)
        total = jnp.sum(wide * wide, axis=1, keepdims=True)
        r = lax.rsqrt(total * (1.0 / head_size) + 1e-06)
        halved = (0.5 * root * root * LOG2E) * total * r * r + 0.5 * math.log2(feats)
        return jnp.exp2(dot(source, dirs, (1, 1)) * (r * (root * LOG2E)) * dir_scale - halved)

    def head(g):
        cols = pl.ds(pl.multiple_of(g * head_size, head_size), head_size)
        dirs, dir_scale = wb[g], scale[g]
        value = vb[:, cols]
        key_map = mapped(kb[:, cols], dirs, dir_scale).astype(BF16)
        t_send[g] = jnp.sum(key_map.astype(F32), axis=0, keepdims=True)
        s_send[g] = dot(key_map, value, (0, 0)).astype(BF16)

        @pl.when(g != g_me)
        def _():
            t_copy(g).start()
            for w in range(EARLY):
                s_copy(g, w).start()

        @pl.when(g == g_me)
        def _():
            s_recv[p_me] = s_send[g]
            t_recv[p_me] = t_send[g]

        query_map = mapped(qb[:, cols], dirs, dir_scale).astype(BF16)
        phi_q[g] = query_map
        scores = jnp.where(causal, dot(query_map, key_map, (1, 1)), 0.0)
        den[g] = jnp.sum(scores, axis=1, keepdims=True)
        num[g] = dot(scores.astype(BF16), value, (1, 0))

    @pl.loop(0, per)
    def _(i):
        head(x * per + i)

    scale_copy(right, x, sc_send.at[0]).wait_recv()
    scale_copy(left, x, sc_send.at[0]).wait_recv()

    @pl.loop(0, 2 * per)
    def _(n):
        side = lax.rem(n, 2)
        i = lax.rem(n // 2 + (per // 2) * side, per)
        slab = step(x, 1 + 2 * side, NX)
        onward = step(x, NX - 1 + 2 * side, NX)
        g = slab * per + i
        feature_copy(wb.at[g], slab, i, x, w_send.at[0, 0]).wait_recv()

        @pl.when(n < per)
        def _():
            feature_copy(wb.at[g], slab, i, onward, wf_send.at[i]).start()

        head(g)

    scale_copy(far, x, sc_send.at[0]).wait_recv()

    @pl.loop(0, per)
    def _(n):
        i = n // 2 + (per // 2) * lax.rem(n, 2)
        g = far * per + i
        feature_copy(wb.at[g], far, i, x, w_send.at[0, 0]).wait_recv()
        head(g)

    for w in range(EARLY, WAVES):
        @pl.loop(1, PLANE)
        def _(k):
            yy, xx = turned(k)
            s_copy(xx * per + yy, w).start()

    def z_copy(w, to):
        return pltpu.make_async_remote_copy(
            src_ref=z_send.at[w], dst_ref=z_recv.at[w, z], send_sem=z_ssem.at[w, to],
            recv_sem=z_rsem.at[w, z], device_id=dev(to, y, x, c), device_id_type=MESH,
        )

    def z_arrival(w, of_z):
        return pltpu.make_async_remote_copy(
            src_ref=z_send.at[w], dst_ref=z_recv.at[w, of_z], send_sem=z_ssem.at[w, of_z],
            recv_sem=z_rsem.at[w, of_z], device_id=dev(of_z, y, x, c), device_id_type=MESH,
        )

    def zt_copy(to, slot):
        return pltpu.make_async_remote_copy(
            src_ref=zt_send, dst_ref=zt_recv.at[slot], send_sem=zt_ssem.at[to],
            recv_sem=zt_rsem.at[slot], device_id=dev(to, y, x, c), device_id_type=MESH,
        )

    def gather(w):
        view = pl.ds(w * part, part)

        @pl.loop(1, PLANE)
        def _(k):
            yy, xx = turned(k)
            p = yy * NX + xx
            pltpu.make_async_remote_copy(
                src_ref=s_send.at[0, view], dst_ref=s_recv.at[p, view], send_sem=s_ssem,
                recv_sem=s_rsem.at[w, p], device_id=dev(z, yy, xx, c), device_id_type=MESH,
            ).wait_recv()
            if w == 0:
                pltpu.make_async_remote_copy(
                    src_ref=t_send.at[0], dst_ref=t_recv.at[p], send_sem=t_ssem,
                    recv_sem=t_rsem.at[p], device_id=dev(z, yy, xx, c), device_id_type=MESH,
                ).wait_recv()

        total = s_recv[0, view].astype(F32)
        for p in range(1, PLANE):
            total = total + s_recv[p, view].astype(F32)
        z_send[w] = total.astype(BF16)
        if w == 0:
            sums = t_recv[0]
            for p in range(1, PLANE):
                sums = sums + t_recv[p]
            zt_send[...] = sums

        @pl.loop(z + 1, NZ)
        def _(to):
            z_copy(w, to).start()
            if w == 0:
                zt_copy(to, z).start()

    def p_copy(w, yy, xx):
        view = pl.ds(w * part, part)
        p = yy * NX + xx
        return pltpu.make_async_remote_copy(
            src_ref=p_send.at[p, view], dst_ref=p_recv.at[g_me, view], send_sem=p_ssem,
            recv_sem=p_rsem.at[w, g_me], device_id=dev(z, yy, xx, c), device_id_type=MESH,
        )

    def pt_copy(yy, xx):
        p = yy * NX + xx
        return pltpu.make_async_remote_copy(
            src_ref=pt_send.at[p], dst_ref=pt_recv.at[g_me], send_sem=pt_ssem,
            recv_sem=pt_rsem.at[g_me], device_id=dev(z, yy, xx, c), device_id_type=MESH,
        )

    def spread(w):
        view = pl.ds(w * part, part)

        def add(n, base):
            z_arrival(w, n).wait_recv()
            return base + z_recv[w, n].astype(F32)

        base = lax.fori_loop(0, z, add, jnp.zeros((part, head_size), F32))
        for p in range(PLANE):
            p_send[p, view] = base.astype(BF16)
            if p < PLANE - 1:
                base = base + s_recv[p, view].astype(F32)
        if w == 0:
            def add_totals(n, sums):
                zt_copy(n, n).wait_recv()
                return sums + zt_recv[n]

            sums = lax.fori_loop(0, z, add_totals, jnp.zeros((1, feats), F32))
            for p in range(PLANE):
                pt_send[p] = sums
                if p < PLANE - 1:
                    sums = sums + t_recv[p]
            pt_recv[g_me] = pt_send[p_me]
        p_recv[g_me, view] = p_send[p_me, view]

        @pl.loop(1, PLANE)
        def _(k):
            yy, xx = turned(k)
            p_copy(w, yy, xx).start()
            if w == 0:
                pt_copy(yy, xx).start()

    for w in range(WAVES + 1):
        if w < WAVES:
            gather(w)
        if w >= 1:
            spread(w - 1)

    def finish(g):
        cols = pl.ds(pl.multiple_of(g * head_size, head_size), head_size)

        @pl.when(g != g_me)
        def _():
            for w in range(WAVES):
                view = pl.ds(w * part, part)
                pltpu.make_async_remote_copy(
                    src_ref=p_send.at[0, view], dst_ref=p_recv.at[g, view], send_sem=p_ssem,
                    recv_sem=p_rsem.at[w, g], device_id=owner(g), device_id_type=MESH,
                ).wait_recv()
            pltpu.make_async_remote_copy(
                src_ref=pt_send.at[0], dst_ref=pt_recv.at[g], send_sem=pt_ssem,
                recv_sem=pt_rsem.at[g], device_id=owner(g), device_id_type=MESH,
            ).wait_recv()

        query_map = phi_q[g]
        top = num[g] + dot(query_map, p_recv[g], (1, 0))
        bottom = den[g] + jnp.sum(query_map.astype(F32) * pt_recv[g], axis=1, keepdims=True)
        ob[:, cols] = (top * (1.0 / bottom)).astype(BF16)

    for n, dx in enumerate((0, 1, 3, 2)):
        slab = step(x, dx, NX)

        @pl.loop(0, per)
        def _(i):
            finish(slab * per + i)

        cols = pl.ds(pl.multiple_of(slab * width, width), width)
        pltpu.make_async_copy(ob.at[my_rows, cols], out_hbm.at[:, columns(slab, c)], o_sem.at[n]).start()
        pltpu.make_async_remote_copy(
            src_ref=ob.at[other_rows, cols], dst_ref=out_hbm.at[:, columns(slab, c)],
            send_sem=o_ssem.at[n], recv_sem=o_rsem.at[slab], device_id=partner, device_id_type=MESH,
        ).start()

    for t in range(3):
        exchanged(t).wait_send()
    for n in range(per):
        for direction, (target, i) in enumerate(((left, n), (right, (n + per // 2) % per))):
            feature_copy(w_hbm.at[i], x, i, target, w_send.at[direction, i]).wait_send()

    @pl.loop(0, per)
    def _(i):
        feature_copy(wb.at[i], 0, i, x, wf_send.at[i]).wait_send()

    for n, target in enumerate((left, right, far)):
        scale_copy(x, target, sc_send.at[n]).wait_send()

    def all_sent(src, dst, sem, recv_sem):
        pltpu.make_async_remote_copy(
            src_ref=src.at[pl.ds(0, PLANE - 1)], dst_ref=dst.at[pl.ds(0, PLANE - 1)], send_sem=sem,
            recv_sem=recv_sem, device_id=partner, device_id_type=MESH,
        ).wait_send()

    all_sent(s_send, s_recv, s_ssem, s_rsem.at[0, 0])
    all_sent(t_send, t_recv, t_ssem, t_rsem.at[0])
    all_sent(p_send, p_recv, p_ssem, p_rsem.at[0, 0])
    all_sent(pt_send, pt_recv, pt_ssem, pt_rsem.at[0])

    @pl.loop(z + 1, NZ)
    def _(to):
        for w in range(WAVES):
            z_copy(w, to).wait_send()
        zt_copy(to, z).wait_send()

    for n, dx in enumerate((0, 1, 3, 2)):
        slab = step(x, dx, NX)
        cols = pl.ds(pl.multiple_of(slab * width, width), width)
        pltpu.make_async_copy(ob.at[my_rows, cols], out_hbm.at[:, columns(slab, c)], o_sem.at[n]).wait()
        done = pltpu.make_async_remote_copy(
            src_ref=ob.at[other_rows, cols], dst_ref=out_hbm.at[:, columns(slab, other)],
            send_sem=o_ssem.at[n], recv_sem=o_rsem.at[slab], device_id=partner, device_id_type=MESH,
        )
        done.wait_send()
        done.wait_recv()


def body(queries, keys, values, features):
    rows, width = queries.shape[1:]
    local_heads, feats, head_size = features.shape
    heads = local_heads * NX
    tokens = 2 * rows
    half = heads * head_size
    dma, vmem = pltpu.SemaphoreType.DMA, pltpu.VMEM
    any_space = pl.BlockSpec(memory_space=pl.ANY)
    state = (heads, feats, head_size)
    sums = (heads, 1, feats)
    out = pl.pallas_call(
        kernel,
        out_shape=jax.ShapeDtypeStruct((rows, width), BF16),
        in_specs=[any_space] * 4,
        out_specs=any_space,
        scratch_shapes=[
            vmem((tokens, half), BF16), vmem((tokens, half), BF16), vmem((tokens, half), BF16),
            vmem(state, BF16), vmem(sums, F32), vmem((heads, tokens, feats), BF16),
            vmem((heads, tokens, head_size), F32), vmem((heads, tokens, 1), F32), vmem((tokens, half), BF16),
            vmem(state, BF16), vmem(state, BF16), vmem(sums, F32), vmem(sums, F32),
            vmem((WAVES, feats // WAVES, head_size), BF16), vmem((WAVES, NZ, feats // WAVES, head_size), BF16),
            vmem((1, feats), F32), vmem((NZ, 1, feats), F32),
            vmem(state, BF16), vmem(state, BF16), vmem(sums, F32), vmem(sums, F32),
            dma((4,)), dma((3,)), dma((3,)), dma((2, local_heads)), dma((heads,)), dma((local_heads,)), dma((3,)), dma((NX,)),
            dma, dma((WAVES, PLANE)), dma, dma((PLANE,)), dma((WAVES, NZ)), dma((WAVES, NZ)), dma((NZ,)), dma((NZ,)),
            dma, dma((WAVES, heads)), dma, dma((heads,)), dma((NX,)), dma((NX,)), dma((NX,)),
        ],
        compiler_params=pltpu.CompilerParams(
            collective_id=0, has_side_effects=True, vmem_limit_bytes=40 * 1024 * 1024
        ),
    )(queries.reshape(rows, width), keys.reshape(rows, width), values.reshape(rows, width), features)
    return out.reshape(1, rows, width)


def solution(mesh):
    tokens = P(None, ("seq", "head"), None)
    return jax.shard_map(
        body, mesh=mesh, in_specs=(tokens, tokens, tokens, P("head", None, None)), out_specs=tokens, check_vma=False
    )
```

```python
import math

import jax
import jax.numpy as jnp
from jax import lax
from jax.experimental import pallas as pl
from jax.experimental.pallas import tpu as pltpu
from jax.sharding import PartitionSpec as P

MESH = pl.DeviceIdType.MESH
NZ, NY, NX = 8, 4, 4
PLANE = NY * NX
WAVES = 4
EARLY = 2
SCHEDULE = "q0 q1 g0 g1 q2 g2 q3 s0 g3 s1 s2 s3".split()
LOG2E = 1.4426950408889634
F32 = jnp.float32
BF16 = jnp.bfloat16


def dot(a, b, contract):
    return lax.dot_general(a, b, ((contract[:1], contract[1:]), ((), ())), preferred_element_type=F32)


def kernel(
    q_hbm, k_hbm, v_hbm, w_hbm, out_hbm,
    qb, kb, vb, wb, scale, phi_q, phi_k, num, den, ob,
    s_send, s_recv, t_send, t_recv, z_send, z_recv, zt_send, zt_recv,
    p_send, p_recv, pt_send, pt_recv,
    in_sem, ex_send, ex_recv, w_send, w_recv, wf_send, wz_send,
    s_ssem, s_rsem, t_ssem, t_rsem, z_ssem, z_rsem, zt_ssem, zt_rsem,
    p_ssem, p_rsem, pt_ssem, pt_rsem, o_sem, o_ssem, o_rsem,
):
    heads, tokens, head_size = num.shape
    feats = wb.shape[1]
    rows = tokens // 2
    per = heads // NX
    width = per * head_size
    part = feats // WAVES
    root = head_size ** (-0.25)

    seq = lax.axis_index("seq")
    pos = lax.axis_index("head")
    z, y = seq // NY, lax.rem(seq, NY)
    x, c = pos // 2, lax.rem(pos, 2)
    p_me = y * NX + x
    g_me = x * per + y
    other = 1 - c

    def dev(zz, yy, xx, cc):
        return (zz * NY + yy, xx * 2 + cc)

    def step(a, d, n):
        return lax.rem(a + d, n)

    def turned(k):
        return step(y, k // NX, NY), step(x, lax.rem(k, NX), NX)

    partner = dev(z, y, x, other)

    barrier = pltpu.get_barrier_semaphore()
    pl.semaphore_signal(barrier, inc=1, device_id=partner, device_id_type=MESH)

    @pl.loop(1, NZ)
    def _(d):
        pl.semaphore_signal(barrier, inc=1, device_id=dev(step(z, d, NZ), y, x, c), device_id_type=MESH)

    @pl.loop(1, PLANE)
    def _(k):
        yy, xx = turned(k)
        pl.semaphore_signal(barrier, inc=1, device_id=dev(z, yy, xx, c), device_id_type=MESH)

    def columns(slab, core):
        return pl.ds(pl.multiple_of((slab * 2 + core) * width, width), width)

    def mine(slab):
        return pl.ds(pl.multiple_of(slab * width, width), width)

    my_rows = pl.ds(pl.multiple_of(c * rows, rows), rows)
    other_rows = pl.ds(pl.multiple_of(other * rows, rows), rows)

    w_local = pltpu.make_async_copy(w_hbm, wb.at[pl.ds(x * per, per)], in_sem.at[3])
    w_local.start()
    pairs = ((k_hbm, kb), (v_hbm, vb), (q_hbm, qb))
    for t, (src, dst) in enumerate(pairs):
        for slab in range(NX):
            pltpu.make_async_copy(src.at[:, columns(slab, c)], dst.at[my_rows, mine(slab)], in_sem.at[t]).start()

    pl.semaphore_wait(barrier, NZ - 1 + PLANE)

    right, left, far = step(x, 1, NX), step(x, NX - 1, NX), step(x, 2, NX)

    even = lax.rem(z, 2)
    up, down = step(z, 1, NZ), step(z, NZ - 1, NZ)
    order = (x, right, left, far)

    def feature_copy(src, g, target, sem):
        return pltpu.make_async_remote_copy(
            src_ref=src, dst_ref=wb.at[g], send_sem=sem, recv_sem=w_recv.at[g],
            device_id=target, device_id_type=MESH,
        )

    def feature_sends():
        for n in range(2):
            for direction, (target, b) in enumerate(((left, n), (right, 1 - n))):
                i = 2 * even + b
                yield feature_copy(w_hbm.at[i], x * per + i, dev(z, y, target, c), w_send.at[direction, b])


    def feature_up(slab, b):
        g = slab * per + 2 * even + b
        return feature_copy(wb.at[g], g, dev(up + (down - up) * b, y, x, c), wz_send.at[slab, b])

    def feature_on(slab, b, target):
        g = slab * per + 2 * even + b
        return feature_copy(wb.at[g], g, dev(z, y, target, c), wf_send.at[b])

    def feature_wait(g):
        feature_copy(wb.at[g], g, partner, w_send.at[0, 0]).wait_recv()

    def exchange(t, n):
        src, dst = pairs[t]
        slab = order[n]
        pltpu.make_async_remote_copy(
            src_ref=src.at[:, columns(slab, other)], dst_ref=dst.at[my_rows, mine(slab)],
            send_sem=ex_send.at[t], recv_sem=ex_recv.at[t, n], device_id=partner, device_id_type=MESH,
        ).start()

    def exchanged(t, n):
        view = pairs[t][1].at[other_rows, mine(order[n])]
        pltpu.make_async_remote_copy(
            src_ref=view, dst_ref=view, send_sem=ex_send.at[t], recv_sem=ex_recv.at[t, n],
            device_id=partner, device_id_type=MESH,
        ).wait_recv()

    for copy in feature_sends():
        copy.start()
    for n in range(NX):
        for t in range(2):
            exchange(t, n)
    for n in range(NX):
        exchange(2, n)
    w_local.wait()
    for t, (src, dst) in enumerate(pairs):
        pltpu.make_async_copy(dst.at[my_rows], dst.at[my_rows], in_sem.at[t]).wait()

    def owner(g):
        return dev(z, lax.rem(g, per), g // per, c)

    def s_copy(g, w):
        view = pl.ds(w * part, part)
        return pltpu.make_async_remote_copy(
            src_ref=s_send.at[g, view], dst_ref=s_recv.at[p_me, view], send_sem=s_ssem,
            recv_sem=s_rsem.at[w, p_me], device_id=owner(g), device_id_type=MESH,
        )

    def t_copy(g):
        return pltpu.make_async_remote_copy(
            src_ref=t_send.at[g], dst_ref=t_recv.at[p_me], send_sem=t_ssem,
            recv_sem=t_rsem.at[p_me], device_id=owner(g), device_id_type=MESH,
        )

    at = lax.broadcasted_iota(jnp.int32, (tokens, tokens), 0)
    of = lax.broadcasted_iota(jnp.int32, (tokens, tokens), 1)
    causal = at >= of

    def mapped(source, dirs, dir_scale):
        wide = source.astype(F32)
        total = jnp.sum(wide * wide, axis=1, keepdims=True)
        r = lax.rsqrt(total * (1.0 / head_size) + 1e-06)
        halved = (0.5 * root * root * LOG2E) * total * r * r + 0.5 * math.log2(feats)
        return jnp.exp2(dot(source, dirs, (1, 1)) * (r * (root * LOG2E)) * dir_scale - halved)

    def head_columns(g):
        return pl.ds(pl.multiple_of(g * head_size, head_size), head_size)

    ones = jnp.ones((8, head_size), BF16)

    def key_parts(gs):
        for g in gs:
            cols = head_columns(g)
            dirs = wb[g]
            square = dirs.astype(F32) * dirs.astype(F32)
            high = square.astype(BF16)
            low = (square - high.astype(F32)).astype(BF16)
            total = dot(ones, high, (1, 1)) + dot(ones, low, (1, 1))
            dir_scale = lax.rsqrt(total[0:1] * (1.0 / head_size) + 1e-06)
            scale[g] = dir_scale
            key_map = mapped(kb[:, cols], dirs, dir_scale).astype(BF16)
            phi_k[g] = key_map
            t_send[g] = jnp.sum(key_map.astype(F32), axis=0, keepdims=True)
            s_send[g] = dot(key_map, vb[:, cols], (0, 0)).astype(BF16)
        for g in gs:
            @pl.when(g != g_me)
            def _():
                t_copy(g).start()
                for w in range(EARLY):
                    s_copy(g, w).start()

            @pl.when(g == g_me)
            def _():
                s_recv[p_me] = s_send[g]
                t_recv[p_me] = t_send[g]

    def query_parts(gs):
        for g in gs:
            cols = head_columns(g)
            query_map = mapped(qb[:, cols], wb[g], scale[g]).astype(BF16)
            phi_q[g] = query_map
            scores = jnp.where(causal, dot(query_map, phi_k[g], (1, 1)), 0.0)
            den[g] = jnp.sum(scores, axis=1, keepdims=True)
            num[g] = dot(scores.astype(BF16), vb[:, cols], (1, 0))

    def queries_of(n):
        exchanged(2, n)

        @pl.loop(0, per, step=2)
        def _(i):
            query_parts([order[n] * per + i, order[n] * per + i + 1])

    def near(n, own):
        side = n % 2
        b = (n // 2 + side) % 2
        slab = (right, left)[side]
        return slab, b, slab * per + 2 * (even if own else 1 - even) + b

    def pass_on(n):
        slab, b, g = near(n, True)
        feature_wait(g)
        if n < 2:
            feature_on(slab, b, (left, right)[n % 2]).start()
        feature_up(slab, b).start()

    def pass_far(b):
        feature_wait(far * per + 2 * even + b)
        feature_up(far, b).start()

    for t in range(2):
        exchanged(t, 0)
    key_parts([x * per, x * per + 1])
    pass_on(0)
    pass_on(1)
    key_parts([x * per + 2, x * per + 3])
    pass_on(2)
    pass_on(3)
    for n in (1, 2):
        for t in range(2):
            exchanged(t, n)
    key_parts([near(0, True)[2], near(1, True)[2]])
    pass_far(0)
    key_parts([near(2, True)[2], near(3, True)[2]])
    pass_far(1)
    for t in range(2):
        exchanged(t, 3)
    key_parts([far * per + 2 * even, far * per + 2 * even + 1])
    late = [near(n, False)[2] for n in range(4)] + [far * per + 2 * (1 - even) + b for b in range(2)]
    for n in range(0, 6, 2):
        feature_wait(late[n])
        feature_wait(late[n + 1])
        key_parts(late[n:n + 2])

    for w in range(EARLY, WAVES):
        @pl.loop(1, PLANE)
        def _(k):
            yy, xx = turned(k)
            s_copy(xx * per + yy, w).start()

    def z_copy(w, to):
        return pltpu.make_async_remote_copy(
            src_ref=z_send.at[w], dst_ref=z_recv.at[w, z], send_sem=z_ssem.at[w, to],
            recv_sem=z_rsem.at[w, z], device_id=dev(to, y, x, c), device_id_type=MESH,
        )

    def z_arrival(w, of_z):
        return pltpu.make_async_remote_copy(
            src_ref=z_send.at[w], dst_ref=z_recv.at[w, of_z], send_sem=z_ssem.at[w, of_z],
            recv_sem=z_rsem.at[w, of_z], device_id=dev(of_z, y, x, c), device_id_type=MESH,
        )

    def zt_copy(to, slot):
        return pltpu.make_async_remote_copy(
            src_ref=zt_send, dst_ref=zt_recv.at[slot], send_sem=zt_ssem.at[to],
            recv_sem=zt_rsem.at[slot], device_id=dev(to, y, x, c), device_id_type=MESH,
        )

    def gather(w):
        view = pl.ds(w * part, part)

        @pl.loop(1, PLANE)
        def _(k):
            yy, xx = turned(k)
            p = yy * NX + xx
            pltpu.make_async_remote_copy(
                src_ref=s_send.at[0, view], dst_ref=s_recv.at[p, view], send_sem=s_ssem,
                recv_sem=s_rsem.at[w, p], device_id=dev(z, yy, xx, c), device_id_type=MESH,
            ).wait_recv()
            if w == 0:
                pltpu.make_async_remote_copy(
                    src_ref=t_send.at[0], dst_ref=t_recv.at[p], send_sem=t_ssem,
                    recv_sem=t_rsem.at[p], device_id=dev(z, yy, xx, c), device_id_type=MESH,
                ).wait_recv()

        total = s_recv[0, view].astype(F32)
        for p in range(1, PLANE):
            total = total + s_recv[p, view].astype(F32)
        z_send[w] = total.astype(BF16)
        if w == 0:
            sums = t_recv[0]
            for p in range(1, PLANE):
                sums = sums + t_recv[p]
            zt_send[...] = sums

        @pl.loop(z + 1, NZ)
        def _(to):
            z_copy(w, to).start()
            if w == 0:
                zt_copy(to, z).start()

    def p_copy(w, yy, xx):
        view = pl.ds(w * part, part)
        p = yy * NX + xx
        return pltpu.make_async_remote_copy(
            src_ref=p_send.at[p, view], dst_ref=p_recv.at[g_me, view], send_sem=p_ssem,
            recv_sem=p_rsem.at[w, g_me], device_id=dev(z, yy, xx, c), device_id_type=MESH,
        )

    def pt_copy(yy, xx):
        p = yy * NX + xx
        return pltpu.make_async_remote_copy(
            src_ref=pt_send.at[p], dst_ref=pt_recv.at[g_me], send_sem=pt_ssem,
            recv_sem=pt_rsem.at[g_me], device_id=dev(z, yy, xx, c), device_id_type=MESH,
        )

    def spread(w):
        view = pl.ds(w * part, part)

        def add(n, base):
            z_arrival(w, n).wait_recv()
            return base + z_recv[w, n].astype(F32)

        base = lax.fori_loop(0, z, add, jnp.zeros((part, head_size), F32))
        for p in range(PLANE):
            p_send[p, view] = base.astype(BF16)
            if p < PLANE - 1:
                base = base + s_recv[p, view].astype(F32)
        if w == 0:
            def add_totals(n, sums):
                zt_copy(n, n).wait_recv()
                return sums + zt_recv[n]

            sums = lax.fori_loop(0, z, add_totals, jnp.zeros((1, feats), F32))
            for p in range(PLANE):
                pt_send[p] = sums
                if p < PLANE - 1:
                    sums = sums + t_recv[p]
            pt_recv[g_me] = pt_send[p_me]
        p_recv[g_me, view] = p_send[p_me, view]

        @pl.loop(1, PLANE)
        def _(k):
            yy, xx = turned(k)
            p_copy(w, yy, xx).start()
            if w == 0:
                pt_copy(yy, xx).start()

    for stage in SCHEDULE:
        kind, n = stage[0], int(stage[1])
        if kind == "q":
            queries_of(n)
        elif kind == "g":
            gather(n)
        else:
            spread(n)

    def arrive(g):
        @pl.when(g != g_me)
        def _():
            for w in range(WAVES):
                view = pl.ds(w * part, part)
                pltpu.make_async_remote_copy(
                    src_ref=p_send.at[0, view], dst_ref=p_recv.at[g, view], send_sem=p_ssem,
                    recv_sem=p_rsem.at[w, g], device_id=owner(g), device_id_type=MESH,
                ).wait_recv()

    def finish(g):
        ob[:, head_columns(g)] = ((num[g] + dot(phi_q[g], p_recv[g], (1, 0))) * den[g]).astype(BF16)

    def normalizer(g):
        @pl.when(g != g_me)
        def _():
            pltpu.make_async_remote_copy(
                src_ref=pt_send.at[0], dst_ref=pt_recv.at[g], send_sem=pt_ssem,
                recv_sem=pt_rsem.at[g], device_id=owner(g), device_id_type=MESH,
            ).wait_recv()

        den[g] = 1.0 / (den[g] + jnp.sum(phi_q[g].astype(F32) * pt_recv[g], axis=1, keepdims=True))

    def out_columns(g, core):
        at_head = (g // per * 2 + core) * per + lax.rem(g, per)
        return pl.ds(pl.multiple_of(at_head * head_size, head_size), head_size)

    def keep(g):
        cols = head_columns(g)
        return pltpu.make_async_copy(ob.at[my_rows, cols], out_hbm.at[:, out_columns(g, c)], o_sem.at[g])

    def give(g):
        cols = head_columns(g)
        return pltpu.make_async_remote_copy(
            src_ref=ob.at[other_rows, cols], dst_ref=out_hbm.at[:, out_columns(g, c)],
            send_sem=o_ssem.at[g], recv_sem=o_rsem.at[g], device_id=partner, device_id_type=MESH,
        )

    @pl.loop(0, heads)
    def _(k):
        normalizer(step(x * per, k, heads))

    @pl.loop(0, heads, step=2)
    def _(k):
        g = step(x * per, k, heads)
        arrive(g)
        arrive(g + 1)
        finish(g)
        finish(g + 1)
        for gg in (g, g + 1):
            give(gg).start()
            keep(gg).start()

    for copy in feature_sends():
        copy.wait_send()
    for b, slab in enumerate((right, left)):
        feature_on(slab, b, x).wait_send()
    for slab in (right, left, far):
        for b in range(2):
            feature_up(slab, b).wait_send()
    for t in range(3):
        view = pairs[t][1].at[other_rows]
        pltpu.make_async_remote_copy(
            src_ref=view, dst_ref=view, send_sem=ex_send.at[t], recv_sem=ex_recv.at[t, 0],
            device_id=partner, device_id_type=MESH,
        ).wait_send()

    def all_sent(src, dst, sem, recv_sem):
        pltpu.make_async_remote_copy(
            src_ref=src.at[pl.ds(0, PLANE - 1)], dst_ref=dst.at[pl.ds(0, PLANE - 1)], send_sem=sem,
            recv_sem=recv_sem, device_id=partner, device_id_type=MESH,
        ).wait_send()

    all_sent(s_send, s_recv, s_ssem, s_rsem.at[0, 0])
    all_sent(t_send, t_recv, t_ssem, t_rsem.at[0])
    all_sent(p_send, p_recv, p_ssem, p_rsem.at[0, 0])
    all_sent(pt_send, pt_recv, pt_ssem, pt_rsem.at[0])

    @pl.loop(z + 1, NZ)
    def _(to):
        for w in range(WAVES):
            z_copy(w, to).wait_send()
        zt_copy(to, z).wait_send()

    @pl.loop(0, heads)
    def _(g):
        keep(g).wait()
        give(g).wait_send()
        arrived = out_hbm.at[:, out_columns(g, other)]
        pltpu.make_async_remote_copy(
            src_ref=ob.at[other_rows, head_columns(g)], dst_ref=arrived,
            send_sem=o_ssem.at[g], recv_sem=o_rsem.at[g], device_id=partner, device_id_type=MESH,
        ).wait_recv()


def body(queries, keys, values, features):
    rows, width = queries.shape[1:]
    local_heads, feats, head_size = features.shape
    heads = local_heads * NX
    tokens = 2 * rows
    half = heads * head_size
    dma, vmem = pltpu.SemaphoreType.DMA, pltpu.VMEM
    any_space = pl.BlockSpec(memory_space=pl.ANY)
    state = (heads, feats, head_size)
    sums = (heads, 1, feats)
    out = pl.pallas_call(
        kernel,
        out_shape=jax.ShapeDtypeStruct((rows, width), BF16),
        in_specs=[any_space] * 4,
        out_specs=any_space,
        scratch_shapes=[
            vmem((tokens, half), BF16), vmem((tokens, half), BF16), vmem((tokens, half), BF16),
            vmem(state, BF16), vmem(sums, F32), vmem((heads, tokens, feats), BF16), vmem((heads, tokens, feats), BF16),
            vmem((heads, tokens, head_size), F32), vmem((heads, tokens, 1), F32), vmem((tokens, half), BF16),
            vmem(state, BF16), vmem(state, BF16), vmem(sums, F32), vmem(sums, F32),
            vmem((WAVES, feats // WAVES, head_size), BF16), vmem((WAVES, NZ, feats // WAVES, head_size), BF16),
            vmem((1, feats), F32), vmem((NZ, 1, feats), F32),
            vmem(state, BF16), vmem(state, BF16), vmem(sums, F32), vmem(sums, F32),
            dma((4,)), dma((3,)), dma((3, NX)), dma((2, 2)), dma((heads,)), dma((2,)), dma((NX, 2)),
            dma, dma((WAVES, PLANE)), dma, dma((PLANE,)), dma((WAVES, NZ)), dma((WAVES, NZ)), dma((NZ,)), dma((NZ,)),
            dma, dma((WAVES, heads)), dma, dma((heads,)), dma((heads,)), dma((heads,)), dma((heads,)),
        ],
        compiler_params=pltpu.CompilerParams(
            collective_id=0, has_side_effects=True, vmem_limit_bytes=40 * 1024 * 1024
        ),
    )(*(pltpu.with_memory_space_constraint(a, pltpu.HBM) for a in (
        queries.reshape(rows, width), keys.reshape(rows, width), values.reshape(rows, width), features)))
    return out.reshape(1, rows, width)


def solution(mesh):
    tokens = P(None, ("seq", "head"), None)
    return jax.shard_map(
        body, mesh=mesh, in_specs=(tokens, tokens, tokens, P("head", None, None)), out_specs=tokens, check_vma=False
    )
```

```python
import math

import jax
import jax.numpy as jnp
from jax import lax
from jax.experimental import pallas as pl
from jax.experimental.pallas import tpu as pltpu
from jax.sharding import PartitionSpec as P

MESH = pl.DeviceIdType.MESH
NZ, NY, NX = 8, 4, 4
PLANE = NY * NX
WAVES = 4
EARLY = 2
SCHEDULE = ("q0", "q1", "g0", "g1", "q2", "s0", "g2", "q3", "s1", "g3", "s2", "s3")
LOG2E = 1.4426950408889634
F32 = jnp.float32
BF16 = jnp.bfloat16


def dot(a, b, contract):
    return lax.dot_general(a, b, ((contract[:1], contract[1:]), ((), ())), preferred_element_type=F32)


def kernel(
    q_hbm, k_hbm, v_hbm, w_hbm, out_hbm,
    qb, kb, vb, wb, scale, phi_q, phi_k, num, den, ob,
    s_send, s_recv, t_send, t_recv, z_send, z_recv, zt_send, zt_recv,
    p_send, p_recv, pt_send, pt_recv,
    in_sem, ex_send, ex_recv, w_send, w_recv, wf_send, wz_send,
    s_ssem, s_rsem, t_ssem, t_rsem, z_ssem, z_rsem, zt_ssem, zt_rsem,
    p_ssem, p_rsem, pt_ssem, pt_rsem, o_sem, o_ssem, o_rsem, rounds,
):
    heads, tokens, head_size = num.shape
    feats = wb.shape[1]
    rows = tokens // 2
    per = heads // NX
    width = per * head_size
    part = feats // WAVES
    root = head_size ** (-0.25)

    seq = lax.axis_index("seq")
    pos = lax.axis_index("head")
    z, y = seq // NY, lax.rem(seq, NY)
    x, c = pos // 2, lax.rem(pos, 2)
    p_me = y * NX + x
    g_me = x * per + y
    other = 1 - c

    def dev(zz, yy, xx, cc):
        return (zz * NY + yy, xx * 2 + cc)

    def step(a, d, n):
        return lax.rem(a + d, n)

    def turned(k):
        return step(y, k // NX, NY), step(x, lax.rem(k, NX), NX)

    partner = dev(z, y, x, other)

    barrier = pltpu.get_barrier_semaphore()
    pl.semaphore_signal(barrier, inc=1, device_id=partner, device_id_type=MESH)

    near_by = [
        dev(step(z, 1, NZ), y, x, c), dev(step(z, NZ - 1, NZ), y, x, c),
        dev(z, step(y, 1, NY), x, c), dev(z, step(y, NY - 1, NY), x, c),
        dev(z, y, step(x, 1, NX), c), dev(z, y, step(x, NX - 1, NX), c),
    ]
    for to in near_by:
        pl.semaphore_signal(barrier, inc=1, device_id=to, device_id_type=MESH)

    def tell(r):
        for to in near_by:
            pl.semaphore_signal(rounds.at[r], inc=1, device_id=to, device_id_type=MESH)

    def hear(r):
        pl.semaphore_wait(rounds.at[r], len(near_by))

    def columns(slab, core):
        return pl.ds(pl.multiple_of((slab * 2 + core) * width, width), width)

    def mine(slab):
        return pl.ds(pl.multiple_of(slab * width, width), width)

    my_rows = pl.ds(pl.multiple_of(c * rows, rows), rows)
    other_rows = pl.ds(pl.multiple_of(other * rows, rows), rows)

    w_local = pltpu.make_async_copy(w_hbm, wb.at[pl.ds(x * per, per)], in_sem.at[3])
    w_local.start()
    pairs = ((k_hbm, kb), (v_hbm, vb), (q_hbm, qb))
    for t, (src, dst) in enumerate(pairs):
        for slab in range(NX):
            pltpu.make_async_copy(src.at[:, columns(slab, c)], dst.at[my_rows, mine(slab)], in_sem.at[t]).start()

    pl.semaphore_wait(barrier, len(near_by) + 1)
    tell(0)

    right, left, far = step(x, 1, NX), step(x, NX - 1, NX), step(x, 2, NX)

    even = lax.rem(z, 2)
    up, down = step(z, 1, NZ), step(z, NZ - 1, NZ)
    order = (x, right, left, far)

    def feature_copy(src, g, target, sem):
        return pltpu.make_async_remote_copy(
            src_ref=src, dst_ref=wb.at[g], send_sem=sem, recv_sem=w_recv.at[g],
            device_id=target, device_id_type=MESH,
        )

    def feature_sends():
        for n in range(2):
            for direction, (target, b) in enumerate(((left, n), (right, 1 - n))):
                i = 2 * even + b
                yield feature_copy(w_hbm.at[i], x * per + i, dev(z, y, target, c), w_send.at[direction, b])


    def feature_up(slab, b):
        g = slab * per + 2 * even + b
        return feature_copy(wb.at[g], g, dev(up + (down - up) * b, y, x, c), wz_send.at[slab, b])

    def feature_on(slab, b, target):
        g = slab * per + 2 * even + b
        return feature_copy(wb.at[g], g, dev(z, y, target, c), wf_send.at[b])

    def feature_wait(g):
        feature_copy(wb.at[g], g, partner, w_send.at[0, 0]).wait_recv()

    def exchange(t, n):
        src, dst = pairs[t]
        slab = order[n]
        pltpu.make_async_remote_copy(
            src_ref=src.at[:, columns(slab, other)], dst_ref=dst.at[my_rows, mine(slab)],
            send_sem=ex_send.at[t], recv_sem=ex_recv.at[t, n], device_id=partner, device_id_type=MESH,
        ).start()

    def exchanged(t, n):
        view = pairs[t][1].at[other_rows, mine(order[n])]
        pltpu.make_async_remote_copy(
            src_ref=view, dst_ref=view, send_sem=ex_send.at[t], recv_sem=ex_recv.at[t, n],
            device_id=partner, device_id_type=MESH,
        ).wait_recv()

    for copy in feature_sends():
        copy.start()
    for n in range(NX):
        for t in range(2):
            exchange(t, n)
    for n in range(NX):
        exchange(2, n)
    w_local.wait()
    for t, (src, dst) in enumerate(pairs):
        pltpu.make_async_copy(dst.at[my_rows], dst.at[my_rows], in_sem.at[t]).wait()

    def owner(g):
        return dev(z, lax.rem(g, per), g // per, c)

    def s_copy(g, w):
        view = pl.ds(w * part, part)
        return pltpu.make_async_remote_copy(
            src_ref=s_send.at[g, view], dst_ref=s_recv.at[p_me, view], send_sem=s_ssem,
            recv_sem=s_rsem.at[w, p_me], device_id=owner(g), device_id_type=MESH,
        )

    def t_copy(g):
        return pltpu.make_async_remote_copy(
            src_ref=t_send.at[g], dst_ref=t_recv.at[p_me], send_sem=t_ssem,
            recv_sem=t_rsem.at[p_me], device_id=owner(g), device_id_type=MESH,
        )

    at = lax.broadcasted_iota(jnp.int32, (tokens, tokens), 0)
    of = lax.broadcasted_iota(jnp.int32, (tokens, tokens), 1)
    causal = at >= of

    def mapped(source, dirs, dir_scale):
        wide = source.astype(F32)
        total = jnp.sum(wide * wide, axis=1, keepdims=True)
        r = lax.rsqrt(total * (1.0 / head_size) + 1e-06)
        halved = (0.5 * root * root * LOG2E) * total * r * r + 0.5 * math.log2(feats)
        return jnp.exp2(dot(source, dirs, (1, 1)) * (r * (root * LOG2E)) * dir_scale - halved)

    def head_columns(g):
        return pl.ds(pl.multiple_of(g * head_size, head_size), head_size)

    ones = jnp.ones((8, head_size), BF16)

    def key_parts(gs):
        for g in gs:
            cols = head_columns(g)
            dirs = wb[g]
            square = dirs.astype(F32) * dirs.astype(F32)
            high = square.astype(BF16)
            low = (square - high.astype(F32)).astype(BF16)
            total = dot(ones, high, (1, 1)) + dot(ones, low, (1, 1))
            dir_scale = lax.rsqrt(total[0:1] * (1.0 / head_size) + 1e-06)
            scale[g] = dir_scale
            key_map = mapped(kb[:, cols], dirs, dir_scale).astype(BF16)
            phi_k[g] = key_map
            t_send[g] = jnp.sum(key_map.astype(F32), axis=0, keepdims=True)
            s_send[g] = dot(key_map, vb[:, cols], (0, 0)).astype(BF16)
        for g in gs:
            @pl.when(g != g_me)
            def _():
                t_copy(g).start()
                for w in range(EARLY):
                    s_copy(g, w).start()

            @pl.when(g == g_me)
            def _():
                s_recv[p_me] = s_send[g]
                t_recv[p_me] = t_send[g]

    def query_parts(gs):
        for g in gs:
            cols = head_columns(g)
            query_map = mapped(qb[:, cols], wb[g], scale[g]).astype(BF16)
            phi_q[g] = query_map
            scores = jnp.where(causal, dot(query_map, phi_k[g], (1, 1)), 0.0)
            den[g] = jnp.sum(scores, axis=1, keepdims=True)
            num[g] = dot(scores.astype(BF16), vb[:, cols], (1, 0))

    def queries_of(n):
        exchanged(2, n)

        @pl.loop(0, per, step=2)
        def _(i):
            query_parts([order[n] * per + i, order[n] * per + i + 1])

    def near(n, own):
        side = n % 2
        b = (n // 2 + side) % 2
        slab = (right, left)[side]
        return slab, b, slab * per + 2 * (even if own else 1 - even) + b

    def pass_on(n):
        slab, b, g = near(n, True)
        feature_wait(g)
        if n < 2:
            feature_on(slab, b, (left, right)[n % 2]).start()
        feature_up(slab, b).start()

    def pass_far(b):
        feature_wait(far * per + 2 * even + b)
        feature_up(far, b).start()

    for t in range(2):
        exchanged(t, 0)
    hear(0)
    tell(1)
    key_parts([x * per, x * per + 1])
    hear(1)
    tell(2)
    pass_on(0)
    pass_on(1)
    key_parts([x * per + 2, x * per + 3])
    pass_on(2)
    pass_on(3)
    for n in (1, 2):
        for t in range(2):
            exchanged(t, n)
    hear(2)
    key_parts([near(0, True)[2], near(1, True)[2]])
    pass_far(0)
    key_parts([near(2, True)[2], near(3, True)[2]])
    pass_far(1)
    for t in range(2):
        exchanged(t, 3)
    key_parts([far * per + 2 * even, far * per + 2 * even + 1])
    late = [near(n, False)[2] for n in range(4)] + [far * per + 2 * (1 - even) + b for b in range(2)]
    for n in range(0, 6, 2):
        feature_wait(late[n])
        feature_wait(late[n + 1])
        key_parts(late[n:n + 2])

    for w in range(EARLY, WAVES):
        @pl.loop(1, PLANE)
        def _(k):
            yy, xx = turned(k)
            s_copy(xx * per + yy, w).start()

    def z_copy(w, to):
        return pltpu.make_async_remote_copy(
            src_ref=z_send.at[w], dst_ref=z_recv.at[w, z], send_sem=z_ssem.at[w, to],
            recv_sem=z_rsem.at[w, z], device_id=dev(to, y, x, c), device_id_type=MESH,
        )

    def z_arrival(w, of_z):
        return pltpu.make_async_remote_copy(
            src_ref=z_send.at[w], dst_ref=z_recv.at[w, of_z], send_sem=z_ssem.at[w, of_z],
            recv_sem=z_rsem.at[w, of_z], device_id=dev(of_z, y, x, c), device_id_type=MESH,
        )

    def zt_copy(to, slot):
        return pltpu.make_async_remote_copy(
            src_ref=zt_send, dst_ref=zt_recv.at[slot], send_sem=zt_ssem.at[to],
            recv_sem=zt_rsem.at[slot], device_id=dev(to, y, x, c), device_id_type=MESH,
        )

    def gather(w):
        view = pl.ds(w * part, part)

        @pl.loop(1, PLANE)
        def _(k):
            yy, xx = turned(k)
            p = yy * NX + xx
            pltpu.make_async_remote_copy(
                src_ref=s_send.at[0, view], dst_ref=s_recv.at[p, view], send_sem=s_ssem,
                recv_sem=s_rsem.at[w, p], device_id=dev(z, yy, xx, c), device_id_type=MESH,
            ).wait_recv()
            if w == 0:
                pltpu.make_async_remote_copy(
                    src_ref=t_send.at[0], dst_ref=t_recv.at[p], send_sem=t_ssem,
                    recv_sem=t_rsem.at[p], device_id=dev(z, yy, xx, c), device_id_type=MESH,
                ).wait_recv()

        total = s_recv[0, view].astype(F32)
        for p in range(1, PLANE):
            total = total + s_recv[p, view].astype(F32)
        z_send[w] = total.astype(BF16)
        if w == 0:
            sums = t_recv[0]
            for p in range(1, PLANE):
                sums = sums + t_recv[p]
            zt_send[...] = sums

        @pl.loop(z + 1, NZ)
        def _(to):
            z_copy(w, to).start()
            if w == 0:
                zt_copy(to, z).start()

    def p_copy(w, yy, xx):
        view = pl.ds(w * part, part)
        p = yy * NX + xx
        return pltpu.make_async_remote_copy(
            src_ref=p_send.at[p, view], dst_ref=p_recv.at[g_me, view], send_sem=p_ssem,
            recv_sem=p_rsem.at[w, g_me], device_id=dev(z, yy, xx, c), device_id_type=MESH,
        )

    def pt_copy(yy, xx):
        p = yy * NX + xx
        return pltpu.make_async_remote_copy(
            src_ref=pt_send.at[p], dst_ref=pt_recv.at[g_me], send_sem=pt_ssem,
            recv_sem=pt_rsem.at[g_me], device_id=dev(z, yy, xx, c), device_id_type=MESH,
        )

    def spread(w):
        view = pl.ds(w * part, part)

        def add(n, base):
            z_arrival(w, n).wait_recv()
            return base + z_recv[w, n].astype(F32)

        base = lax.fori_loop(0, z, add, jnp.zeros((part, head_size), F32))
        for p in range(PLANE):
            p_send[p, view] = base.astype(BF16)
            if p < PLANE - 1:
                base = base + s_recv[p, view].astype(F32)
        if w == 0:
            def add_totals(n, sums):
                zt_copy(n, n).wait_recv()
                return sums + zt_recv[n]

            sums = lax.fori_loop(0, z, add_totals, jnp.zeros((1, feats), F32))
            for p in range(PLANE):
                pt_send[p] = sums
                if p < PLANE - 1:
                    sums = sums + t_recv[p]
            pt_recv[g_me] = pt_send[p_me]
        p_recv[g_me, view] = p_send[p_me, view]

        @pl.loop(1, PLANE)
        def _(k):
            yy, xx = turned(k)
            p_copy(w, yy, xx).start()
            if w == 0:
                pt_copy(yy, xx).start()

    for stage in SCHEDULE:
        kind, n = stage[0], int(stage[1])
        if kind == "q":
            queries_of(n)
        elif kind == "g":
            gather(n)
        else:
            spread(n)

    def arrive(g):
        @pl.when(g != g_me)
        def _():
            for w in range(WAVES):
                view = pl.ds(w * part, part)
                pltpu.make_async_remote_copy(
                    src_ref=p_send.at[0, view], dst_ref=p_recv.at[g, view], send_sem=p_ssem,
                    recv_sem=p_rsem.at[w, g], device_id=owner(g), device_id_type=MESH,
                ).wait_recv()

    def finish(g):
        ob[:, head_columns(g)] = ((num[g] + dot(phi_q[g], p_recv[g], (1, 0))) * den[g]).astype(BF16)

    def normalizer(g):
        @pl.when(g != g_me)
        def _():
            pltpu.make_async_remote_copy(
                src_ref=pt_send.at[0], dst_ref=pt_recv.at[g], send_sem=pt_ssem,
                recv_sem=pt_rsem.at[g], device_id=owner(g), device_id_type=MESH,
            ).wait_recv()

        den[g] = 1.0 / (den[g] + jnp.sum(phi_q[g].astype(F32) * pt_recv[g], axis=1, keepdims=True))

    def out_columns(g, core):
        at_head = (g // per * 2 + core) * per + lax.rem(g, per)
        return pl.ds(pl.multiple_of(at_head * head_size, head_size), head_size)

    def keep(g):
        cols = head_columns(g)
        return pltpu.make_async_copy(ob.at[my_rows, cols], out_hbm.at[:, out_columns(g, c)], o_sem.at[g])

    def give(g):
        cols = head_columns(g)
        return pltpu.make_async_remote_copy(
            src_ref=ob.at[other_rows, cols], dst_ref=out_hbm.at[:, out_columns(g, c)],
            send_sem=o_ssem.at[g], recv_sem=o_rsem.at[g], device_id=partner, device_id_type=MESH,
        )

    @pl.loop(0, heads)
    def _(k):
        normalizer(step(x * per, k, heads))

    @pl.loop(0, heads, step=2)
    def _(k):
        g = step(x * per, k, heads)
        arrive(g)
        arrive(g + 1)
        finish(g)
        finish(g + 1)
        for gg in (g, g + 1):
            give(gg).start()
            keep(gg).start()

    for copy in feature_sends():
        copy.wait_send()
    for b, slab in enumerate((right, left)):
        feature_on(slab, b, x).wait_send()
    for slab in (right, left, far):
        for b in range(2):
            feature_up(slab, b).wait_send()
    for t in range(3):
        view = pairs[t][1].at[other_rows]
        pltpu.make_async_remote_copy(
            src_ref=view, dst_ref=view, send_sem=ex_send.at[t], recv_sem=ex_recv.at[t, 0],
            device_id=partner, device_id_type=MESH,
        ).wait_send()

    def all_sent(src, dst, sem, recv_sem):
        pltpu.make_async_remote_copy(
            src_ref=src.at[pl.ds(0, PLANE - 1)], dst_ref=dst.at[pl.ds(0, PLANE - 1)], send_sem=sem,
            recv_sem=recv_sem, device_id=partner, device_id_type=MESH,
        ).wait_send()

    all_sent(s_send, s_recv, s_ssem, s_rsem.at[0, 0])
    all_sent(t_send, t_recv, t_ssem, t_rsem.at[0])
    all_sent(p_send, p_recv, p_ssem, p_rsem.at[0, 0])
    all_sent(pt_send, pt_recv, pt_ssem, pt_rsem.at[0])

    @pl.loop(z + 1, NZ)
    def _(to):
        for w in range(WAVES):
            z_copy(w, to).wait_send()
        zt_copy(to, z).wait_send()

    @pl.loop(0, heads)
    def _(g):
        keep(g).wait()
        give(g).wait_send()
        arrived = out_hbm.at[:, out_columns(g, other)]
        pltpu.make_async_remote_copy(
            src_ref=ob.at[other_rows, head_columns(g)], dst_ref=arrived,
            send_sem=o_ssem.at[g], recv_sem=o_rsem.at[g], device_id=partner, device_id_type=MESH,
        ).wait_recv()


def body(queries, keys, values, features):
    rows, width = queries.shape[1:]
    local_heads, feats, head_size = features.shape
    heads = local_heads * NX
    tokens = 2 * rows
    half = heads * head_size
    dma, vmem = pltpu.SemaphoreType.DMA, pltpu.VMEM
    any_space = pl.BlockSpec(memory_space=pl.ANY)
    state = (heads, feats, head_size)
    sums = (heads, 1, feats)
    out = pl.pallas_call(
        kernel,
        out_shape=jax.ShapeDtypeStruct((rows, width), BF16),
        in_specs=[any_space] * 4,
        out_specs=any_space,
        scratch_shapes=[
            vmem((tokens, half), BF16), vmem((tokens, half), BF16), vmem((tokens, half), BF16),
            vmem(state, BF16), vmem(sums, F32), vmem((heads, tokens, feats), BF16), vmem((heads, tokens, feats), BF16),
            vmem((heads, tokens, head_size), F32), vmem((heads, tokens, 1), F32), vmem((tokens, half), BF16),
            vmem(state, BF16), vmem(state, BF16), vmem(sums, F32), vmem(sums, F32),
            vmem((WAVES, feats // WAVES, head_size), BF16), vmem((WAVES, NZ, feats // WAVES, head_size), BF16),
            vmem((1, feats), F32), vmem((NZ, 1, feats), F32),
            vmem(state, BF16), vmem(state, BF16), vmem(sums, F32), vmem(sums, F32),
            dma((4,)), dma((3,)), dma((3, NX)), dma((2, 2)), dma((heads,)), dma((2,)), dma((NX, 2)),
            dma, dma((WAVES, PLANE)), dma, dma((PLANE,)), dma((WAVES, NZ)), dma((WAVES, NZ)), dma((NZ,)), dma((NZ,)),
            dma, dma((WAVES, heads)), dma, dma((heads,)), dma((heads,)), dma((heads,)), dma((heads,)),
            pltpu.SemaphoreType.REGULAR((3,)),
        ],
        compiler_params=pltpu.CompilerParams(
            collective_id=0, has_side_effects=True, vmem_limit_bytes=40 * 1024 * 1024
        ),
    )(*(pltpu.with_memory_space_constraint(a, pltpu.HBM) for a in (
        queries.reshape(rows, width), keys.reshape(rows, width), values.reshape(rows, width), features)))
    return out.reshape(1, rows, width)


def solution(mesh):
    tokens = P(None, ("seq", "head"), None)
    return jax.shard_map(
        body, mesh=mesh, in_specs=(tokens, tokens, tokens, P("head", None, None)), out_specs=tokens, check_vma=False
    )
```

```python
import math

import jax
import jax.numpy as jnp
from jax import lax
from jax.experimental import pallas as pl
from jax.experimental.pallas import tpu as pltpu
from jax.sharding import PartitionSpec as P

MESH = pl.DeviceIdType.MESH
NZ, NY, NX = 8, 4, 4
PLANE = NY * NX
PARTS = (5, 5, 6)
WAVES = len(PARTS)
EARLY = 2
SCHEDULE = ("q0", "q1", "g0", "g1", "q2", "s0", "g2", "q3", "s1", "s2")
LOG2E = 1.4426950408889634
F32 = jnp.float32
BF16 = jnp.bfloat16


def dot(a, b, contract):
    return lax.dot_general(a, b, ((contract[:1], contract[1:]), ((), ())), preferred_element_type=F32)


def kernel(
    q_hbm, k_hbm, v_hbm, w_hbm, out_hbm,
    qb, kb, vb, wb, scale, phi_q, phi_k, num, den, ob,
    s_send, s_recv, t_send, t_recv, z_send, z_recv, zt_send, zt_recv,
    p_send, p_recv, pt_send, pt_recv,
    in_sem, ex_send, ex_recv, w_send, w_recv, wf_send, wz_send,
    s_ssem, s_rsem, t_ssem, t_rsem, z_ssem, z_rsem, zt_ssem, zt_rsem,
    p_ssem, p_rsem, pt_ssem, pt_rsem, o_sem, o_ssem, o_rsem, rounds,
):
    heads, tokens, head_size = num.shape
    feats = wb.shape[1]
    rows = tokens // 2
    per = heads // NX
    width = per * head_size
    starts = [feats * sum(PARTS[:w]) // sum(PARTS) for w in range(WAVES + 1)]
    root = head_size ** (-0.25)

    seq = lax.axis_index("seq")
    pos = lax.axis_index("head")
    z, y = seq // NY, lax.rem(seq, NY)
    x, c = pos // 2, lax.rem(pos, 2)
    p_me = y * NX + x
    g_me = x * per + y
    other = 1 - c

    def dev(zz, yy, xx, cc):
        return (zz * NY + yy, xx * 2 + cc)

    def piece(w):
        return pl.ds(starts[w], starts[w + 1] - starts[w])

    def step(a, d, n):
        return lax.rem(a + d, n)

    def turned(k):
        return step(y, k // NX, NY), step(x, lax.rem(k, NX), NX)

    partner = dev(z, y, x, other)

    barrier = pltpu.get_barrier_semaphore()
    pl.semaphore_signal(barrier, inc=1, device_id=partner, device_id_type=MESH)

    near_by = [
        dev(step(z, 1, NZ), y, x, c), dev(step(z, NZ - 1, NZ), y, x, c),
        dev(z, step(y, 1, NY), x, c), dev(z, step(y, NY - 1, NY), x, c),
        dev(z, y, step(x, 1, NX), c), dev(z, y, step(x, NX - 1, NX), c),
    ]
    for to in near_by:
        pl.semaphore_signal(barrier, inc=1, device_id=to, device_id_type=MESH)

    def tell(r):
        for to in near_by:
            pl.semaphore_signal(rounds.at[r], inc=1, device_id=to, device_id_type=MESH)

    def hear(r):
        pl.semaphore_wait(rounds.at[r], len(near_by))

    def columns(slab, core):
        return pl.ds(pl.multiple_of((slab * 2 + core) * width, width), width)

    def mine(slab):
        return pl.ds(pl.multiple_of(slab * width, width), width)

    my_rows = pl.ds(pl.multiple_of(c * rows, rows), rows)
    other_rows = pl.ds(pl.multiple_of(other * rows, rows), rows)

    w_local = pltpu.make_async_copy(w_hbm, wb.at[pl.ds(x * per, per)], in_sem.at[3])
    w_local.start()
    pairs = ((k_hbm, kb), (v_hbm, vb), (q_hbm, qb))
    for t, (src, dst) in enumerate(pairs):
        for slab in range(NX):
            pltpu.make_async_copy(src.at[:, columns(slab, c)], dst.at[my_rows, mine(slab)], in_sem.at[t]).start()

    pl.semaphore_wait(barrier, len(near_by) + 1)
    tell(0)

    right, left, far = step(x, 1, NX), step(x, NX - 1, NX), step(x, 2, NX)

    even = lax.rem(z, 2)
    up, down = step(z, 1, NZ), step(z, NZ - 1, NZ)
    order = (x, right, left, far)

    def feature_copy(src, g, target, sem):
        return pltpu.make_async_remote_copy(
            src_ref=src, dst_ref=wb.at[g], send_sem=sem, recv_sem=w_recv.at[g],
            device_id=target, device_id_type=MESH,
        )

    def feature_sends():
        for n in range(2):
            for direction, (target, b) in enumerate(((left, n), (right, 1 - n))):
                i = 2 * even + b
                yield feature_copy(w_hbm.at[i], x * per + i, dev(z, y, target, c), w_send.at[direction, b])


    def feature_up(slab, b):
        g = slab * per + 2 * even + b
        return feature_copy(wb.at[g], g, dev(up + (down - up) * b, y, x, c), wz_send.at[slab, b])

    def feature_on(slab, b, target):
        g = slab * per + 2 * even + b
        return feature_copy(wb.at[g], g, dev(z, y, target, c), wf_send.at[b])

    def feature_wait(g):
        feature_copy(wb.at[g], g, partner, w_send.at[0, 0]).wait_recv()

    def exchange(t, n):
        src, dst = pairs[t]
        slab = order[n]
        pltpu.make_async_remote_copy(
            src_ref=src.at[:, columns(slab, other)], dst_ref=dst.at[my_rows, mine(slab)],
            send_sem=ex_send.at[t], recv_sem=ex_recv.at[t, n], device_id=partner, device_id_type=MESH,
        ).start()

    def exchanged(t, n):
        view = pairs[t][1].at[other_rows, mine(order[n])]
        pltpu.make_async_remote_copy(
            src_ref=view, dst_ref=view, send_sem=ex_send.at[t], recv_sem=ex_recv.at[t, n],
            device_id=partner, device_id_type=MESH,
        ).wait_recv()

    for copy in feature_sends():
        copy.start()
    for n in range(NX):
        for t in range(2):
            exchange(t, n)
    for n in range(NX):
        exchange(2, n)
    w_local.wait()
    for t, (src, dst) in enumerate(pairs):
        pltpu.make_async_copy(dst.at[my_rows], dst.at[my_rows], in_sem.at[t]).wait()

    def owner(g):
        return dev(z, lax.rem(g, per), g // per, c)

    def s_copy(g, w):
        view = piece(w)
        return pltpu.make_async_remote_copy(
            src_ref=s_send.at[g, view], dst_ref=s_recv.at[p_me, view], send_sem=s_ssem,
            recv_sem=s_rsem.at[w, p_me], device_id=owner(g), device_id_type=MESH,
        )

    def t_copy(g):
        return pltpu.make_async_remote_copy(
            src_ref=t_send.at[g], dst_ref=t_recv.at[p_me], send_sem=t_ssem,
            recv_sem=t_rsem.at[p_me], device_id=owner(g), device_id_type=MESH,
        )

    at = lax.broadcasted_iota(jnp.int32, (tokens, tokens), 0)
    of = lax.broadcasted_iota(jnp.int32, (tokens, tokens), 1)
    causal = at >= of

    def mapped(source, dirs, dir_scale):
        wide = source.astype(F32)
        total = jnp.sum(wide * wide, axis=1, keepdims=True)
        r = lax.rsqrt(total * (1.0 / head_size) + 1e-06)
        halved = (0.5 * root * root * LOG2E) * total * r * r + 0.5 * math.log2(feats)
        return jnp.exp2(dot(source, dirs, (1, 1)) * (r * (root * LOG2E)) * dir_scale - halved)

    def head_columns(g):
        return pl.ds(pl.multiple_of(g * head_size, head_size), head_size)

    ones = jnp.ones((8, head_size), BF16)

    def key_parts(gs, early=EARLY):
        for g in gs:
            cols = head_columns(g)
            dirs = wb[g]
            square = dirs.astype(F32) * dirs.astype(F32)
            high = square.astype(BF16)
            low = (square - high.astype(F32)).astype(BF16)
            total = dot(ones, high, (1, 1)) + dot(ones, low, (1, 1))
            dir_scale = lax.rsqrt(total[0:1] * (1.0 / head_size) + 1e-06)
            scale[g] = dir_scale
            key_map = mapped(kb[:, cols], dirs, dir_scale).astype(BF16)
            phi_k[g] = key_map
            t_send[g] = jnp.sum(key_map.astype(F32), axis=0, keepdims=True)
            s_send[g] = dot(key_map, vb[:, cols], (0, 0)).astype(BF16)
        for g in gs:
            @pl.when(g != g_me)
            def _():
                t_copy(g).start()
                for w in range(early):
                    s_copy(g, w).start()

            @pl.when(g == g_me)
            def _():
                s_recv[p_me] = s_send[g]
                t_recv[p_me] = t_send[g]

    def query_parts(gs):
        for g in gs:
            cols = head_columns(g)
            query_map = mapped(qb[:, cols], wb[g], scale[g]).astype(BF16)
            phi_q[g] = query_map
            scores = jnp.where(causal, dot(query_map, phi_k[g], (1, 1)), 0.0)
            den[g] = jnp.sum(scores, axis=1, keepdims=True)
            num[g] = dot(scores.astype(BF16), vb[:, cols], (1, 0))

    def queries_of(n):
        exchanged(2, n)

        @pl.loop(0, per, step=2)
        def _(i):
            query_parts([order[n] * per + i, order[n] * per + i + 1])

    def near(n, own):
        side = n % 2
        b = (n // 2 + side) % 2
        slab = (right, left)[side]
        return slab, b, slab * per + 2 * (even if own else 1 - even) + b

    def pass_on(n):
        slab, b, g = near(n, True)
        feature_wait(g)
        if n < 2:
            feature_on(slab, b, (left, right)[n % 2]).start()
        feature_up(slab, b).start()

    def pass_far(b):
        feature_wait(far * per + 2 * even + b)
        feature_up(far, b).start()

    for t in range(2):
        exchanged(t, 0)
    hear(0)
    tell(1)
    key_parts([x * per, x * per + 1], WAVES)
    hear(1)
    tell(2)
    pass_on(0)
    pass_on(1)
    key_parts([x * per + 2, x * per + 3], WAVES)
    pass_on(2)
    pass_on(3)
    for n in (1, 2):
        for t in range(2):
            exchanged(t, n)
    hear(2)
    key_parts([near(0, True)[2], near(1, True)[2]])
    pass_far(0)
    key_parts([near(2, True)[2], near(3, True)[2]])
    pass_far(1)
    for t in range(2):
        exchanged(t, 3)
    key_parts([far * per + 2 * even, far * per + 2 * even + 1])
    late = [near(n, False)[2] for n in range(4)] + [far * per + 2 * (1 - even) + b for b in range(2)]
    for n in range(0, 6, 2):
        feature_wait(late[n])
        feature_wait(late[n + 1])
        key_parts(late[n:n + 2])

    for w in range(EARLY, WAVES):
        for dx in (1, 3, 2):
            @pl.loop(0, per)
            def _(dy):
                s_copy(step(x, dx, NX) * per + step(y, dy, NY), w).start()

    def z_copy(w, to):
        return pltpu.make_async_remote_copy(
            src_ref=z_send.at[piece(w)], dst_ref=z_recv.at[z, piece(w)], send_sem=z_ssem.at[w, to],
            recv_sem=z_rsem.at[w, z], device_id=dev(to, y, x, c), device_id_type=MESH,
        )

    def z_arrival(w, of_z):
        return pltpu.make_async_remote_copy(
            src_ref=z_send.at[piece(w)], dst_ref=z_recv.at[of_z, piece(w)], send_sem=z_ssem.at[w, of_z],
            recv_sem=z_rsem.at[w, of_z], device_id=dev(of_z, y, x, c), device_id_type=MESH,
        )

    def zt_copy(to, slot):
        return pltpu.make_async_remote_copy(
            src_ref=zt_send, dst_ref=zt_recv.at[slot], send_sem=zt_ssem.at[to],
            recv_sem=zt_rsem.at[slot], device_id=dev(to, y, x, c), device_id_type=MESH,
        )

    def gather(w):
        view = piece(w)

        @pl.loop(1, PLANE)
        def _(k):
            yy, xx = turned(k)
            p = yy * NX + xx
            pltpu.make_async_remote_copy(
                src_ref=s_send.at[0, view], dst_ref=s_recv.at[p, view], send_sem=s_ssem,
                recv_sem=s_rsem.at[w, p], device_id=dev(z, yy, xx, c), device_id_type=MESH,
            ).wait_recv()
            if w == 0:
                pltpu.make_async_remote_copy(
                    src_ref=t_send.at[0], dst_ref=t_recv.at[p], send_sem=t_ssem,
                    recv_sem=t_rsem.at[p], device_id=dev(z, yy, xx, c), device_id_type=MESH,
                ).wait_recv()

        total = s_recv[0, view].astype(F32)
        for p in range(1, PLANE):
            total = total + s_recv[p, view].astype(F32)
        z_send[piece(w)] = total.astype(BF16)
        if w == 0:
            sums = t_recv[0]
            for p in range(1, PLANE):
                sums = sums + t_recv[p]
            zt_send[...] = sums

        @pl.loop(z + 1, NZ)
        def _(to):
            z_copy(w, to).start()
            if w == 0:
                zt_copy(to, z).start()

    def p_copy(w, yy, xx):
        view = piece(w)
        p = yy * NX + xx
        return pltpu.make_async_remote_copy(
            src_ref=p_send.at[p, view], dst_ref=p_recv.at[g_me, view], send_sem=p_ssem,
            recv_sem=p_rsem.at[w, g_me], device_id=dev(z, yy, xx, c), device_id_type=MESH,
        )

    def pt_copy(yy, xx):
        p = yy * NX + xx
        return pltpu.make_async_remote_copy(
            src_ref=pt_send.at[p], dst_ref=pt_recv.at[g_me], send_sem=pt_ssem,
            recv_sem=pt_rsem.at[g_me], device_id=dev(z, yy, xx, c), device_id_type=MESH,
        )

    def spread(w):
        view = piece(w)

        def add(n, base):
            z_arrival(w, n).wait_recv()
            return base + z_recv[n, piece(w)].astype(F32)

        base = lax.fori_loop(0, z, add, jnp.zeros((starts[w + 1] - starts[w], head_size), F32))
        for p in range(PLANE):
            p_send[p, view] = base.astype(BF16)
            if p < PLANE - 1:
                base = base + s_recv[p, view].astype(F32)
        if w == 0:
            def add_totals(n, sums):
                zt_copy(n, n).wait_recv()
                return sums + zt_recv[n]

            sums = lax.fori_loop(0, z, add_totals, jnp.zeros((1, feats), F32))
            for p in range(PLANE):
                pt_send[p] = sums
                if p < PLANE - 1:
                    sums = sums + t_recv[p]
            pt_recv[g_me] = pt_send[p_me]
        p_recv[g_me, view] = p_send[p_me, view]

        @pl.loop(1, PLANE)
        def _(k):
            yy, xx = turned(k)
            p_copy(w, yy, xx).start()
            if w == 0:
                pt_copy(yy, xx).start()

    for stage in SCHEDULE:
        kind, n = stage[0], int(stage[1])
        if kind == "q":
            queries_of(n)
        elif kind == "g":
            gather(n)
        else:
            spread(n)

    def arrive(g):
        @pl.when(g != g_me)
        def _():
            for w in range(WAVES):
                view = piece(w)
                pltpu.make_async_remote_copy(
                    src_ref=p_send.at[0, view], dst_ref=p_recv.at[g, view], send_sem=p_ssem,
                    recv_sem=p_rsem.at[w, g], device_id=owner(g), device_id_type=MESH,
                ).wait_recv()

    def finish(g):
        ob[:, head_columns(g)] = ((num[g] + dot(phi_q[g], p_recv[g], (1, 0))) * den[g]).astype(BF16)

    def normalizer(g):
        @pl.when(g != g_me)
        def _():
            pltpu.make_async_remote_copy(
                src_ref=pt_send.at[0], dst_ref=pt_recv.at[g], send_sem=pt_ssem,
                recv_sem=pt_rsem.at[g], device_id=owner(g), device_id_type=MESH,
            ).wait_recv()

        den[g] = 1.0 / (den[g] + jnp.sum(phi_q[g].astype(F32) * pt_recv[g], axis=1, keepdims=True))

    def out_columns(g, core):
        at_head = (g // per * 2 + core) * per + lax.rem(g, per)
        return pl.ds(pl.multiple_of(at_head * head_size, head_size), head_size)

    def keep(g):
        cols = head_columns(g)
        return pltpu.make_async_copy(ob.at[my_rows, cols], out_hbm.at[:, out_columns(g, c)], o_sem.at[g])

    def give(g):
        cols = head_columns(g)
        return pltpu.make_async_remote_copy(
            src_ref=ob.at[other_rows, cols], dst_ref=out_hbm.at[:, out_columns(g, c)],
            send_sem=o_ssem.at[g], recv_sem=o_rsem.at[g], device_id=partner, device_id_type=MESH,
        )

    @pl.loop(0, heads)
    def _(k):
        normalizer(step(x * per, k, heads))

    @pl.loop(0, heads, step=2)
    def _(k):
        g = step(x * per, k, heads)
        arrive(g)
        arrive(g + 1)
        finish(g)
        finish(g + 1)
        for gg in (g, g + 1):
            give(gg).start()
            keep(gg).start()

    for copy in feature_sends():
        copy.wait_send()
    for b, slab in enumerate((right, left)):
        feature_on(slab, b, x).wait_send()
    for slab in (right, left, far):
        for b in range(2):
            feature_up(slab, b).wait_send()
    for t in range(3):
        view = pairs[t][1].at[other_rows]
        pltpu.make_async_remote_copy(
            src_ref=view, dst_ref=view, send_sem=ex_send.at[t], recv_sem=ex_recv.at[t, 0],
            device_id=partner, device_id_type=MESH,
        ).wait_send()

    def all_sent(src, dst, sem, recv_sem):
        pltpu.make_async_remote_copy(
            src_ref=src.at[pl.ds(0, PLANE - 1)], dst_ref=dst.at[pl.ds(0, PLANE - 1)], send_sem=sem,
            recv_sem=recv_sem, device_id=partner, device_id_type=MESH,
        ).wait_send()

    all_sent(s_send, s_recv, s_ssem, s_rsem.at[0, 0])
    all_sent(t_send, t_recv, t_ssem, t_rsem.at[0])
    all_sent(p_send, p_recv, p_ssem, p_rsem.at[0, 0])
    all_sent(pt_send, pt_recv, pt_ssem, pt_rsem.at[0])

    @pl.loop(z + 1, NZ)
    def _(to):
        for w in range(WAVES):
            z_copy(w, to).wait_send()
        zt_copy(to, z).wait_send()

    @pl.loop(0, heads)
    def _(g):
        keep(g).wait()
        give(g).wait_send()
        arrived = out_hbm.at[:, out_columns(g, other)]
        pltpu.make_async_remote_copy(
            src_ref=ob.at[other_rows, head_columns(g)], dst_ref=arrived,
            send_sem=o_ssem.at[g], recv_sem=o_rsem.at[g], device_id=partner, device_id_type=MESH,
        ).wait_recv()


def body(queries, keys, values, features):
    rows, width = queries.shape[1:]
    local_heads, feats, head_size = features.shape
    heads = local_heads * NX
    tokens = 2 * rows
    half = heads * head_size
    dma, vmem = pltpu.SemaphoreType.DMA, pltpu.VMEM
    any_space = pl.BlockSpec(memory_space=pl.ANY)
    state = (heads, feats, head_size)
    sums = (heads, 1, feats)
    out = pl.pallas_call(
        kernel,
        out_shape=jax.ShapeDtypeStruct((rows, width), BF16),
        in_specs=[any_space] * 4,
        out_specs=any_space,
        scratch_shapes=[
            vmem((tokens, half), BF16), vmem((tokens, half), BF16), vmem((tokens, half), BF16),
            vmem(state, BF16), vmem(sums, F32), vmem((heads, tokens, feats), BF16), vmem((heads, tokens, feats), BF16),
            vmem((heads, tokens, head_size), F32), vmem((heads, tokens, 1), F32), vmem((tokens, half), BF16),
            vmem(state, BF16), vmem(state, BF16), vmem(sums, F32), vmem(sums, F32),
            vmem((feats, head_size), BF16), vmem((NZ, feats, head_size), BF16),
            vmem((1, feats), F32), vmem((NZ, 1, feats), F32),
            vmem(state, BF16), vmem(state, BF16), vmem(sums, F32), vmem(sums, F32),
            dma((4,)), dma((3,)), dma((3, NX)), dma((2, 2)), dma((heads,)), dma((2,)), dma((NX, 2)),
            dma, dma((WAVES, PLANE)), dma, dma((PLANE,)), dma((WAVES, NZ)), dma((WAVES, NZ)), dma((NZ,)), dma((NZ,)),
            dma, dma((WAVES, heads)), dma, dma((heads,)), dma((heads,)), dma((heads,)), dma((heads,)),
            pltpu.SemaphoreType.REGULAR((3,)),
        ],
        compiler_params=pltpu.CompilerParams(
            collective_id=0, has_side_effects=True, vmem_limit_bytes=40 * 1024 * 1024
        ),
    )(*(pltpu.with_memory_space_constraint(a, pltpu.HBM) for a in (
        queries.reshape(rows, width), keys.reshape(rows, width), values.reshape(rows, width), features)))
    return out.reshape(1, rows, width)


def solution(mesh):
    tokens = P(None, ("seq", "head"), None)
    return jax.shard_map(
        body, mesh=mesh, in_specs=(tokens, tokens, tokens, P("head", None, None)), out_specs=tokens, check_vma=False
    )
```

```python
import math

import jax
import jax.numpy as jnp
from jax import lax
from jax.experimental import pallas as pl
from jax.experimental.pallas import tpu as pltpu
from jax.sharding import PartitionSpec as P

MESH = pl.DeviceIdType.MESH
NZ, NY, NX = 8, 4, 4
PLANE = NY * NX
PARTS = (5, 5, 6)
WAVES = len(PARTS)
EARLY = 2
SCHEDULE = ("q0", "q1", "g0", "g1", "s0", "g2", "q2", "s1", "q3", "s2")
LOG2E = 1.4426950408889634
F32 = jnp.float32
BF16 = jnp.bfloat16


def dot(a, b, contract):
    return lax.dot_general(a, b, ((contract[:1], contract[1:]), ((), ())), preferred_element_type=F32)


def kernel(
    q_hbm, k_hbm, v_hbm, w_hbm, out_hbm,
    qb, kb, vb, wb, scale, phi_q, phi_k, num, den, ob,
    s_send, s_recv, t_send, t_recv, z_send, z_recv, zt_send, zt_recv,
    p_send, p_recv, pt_send, pt_recv,
    in_sem, ex_send, ex_recv, w_send, w_recv, wf_send, wz_send,
    s_ssem, s_rsem, t_ssem, t_rsem, z_ssem, z_rsem, zt_ssem, zt_rsem,
    p_ssem, p_rsem, pt_ssem, pt_rsem, o_sem, o_ssem, o_rsem, rounds,
):
    heads, tokens, head_size = num.shape
    feats = wb.shape[1]
    rows = tokens // 2
    per = heads // NX
    width = per * head_size
    starts = [feats * sum(PARTS[:w]) // sum(PARTS) for w in range(WAVES + 1)]
    root = head_size ** (-0.25)

    seq = lax.axis_index("seq")
    pos = lax.axis_index("head")
    z, y = seq // NY, lax.rem(seq, NY)
    x, c = pos // 2, lax.rem(pos, 2)
    p_me = y * NX + x
    g_me = x * per + y
    other = 1 - c

    def dev(zz, yy, xx, cc):
        return (zz * NY + yy, xx * 2 + cc)

    def piece(w):
        return pl.ds(starts[w], starts[w + 1] - starts[w])

    def step(a, d, n):
        return lax.rem(a + d, n)

    def turned(k):
        return step(y, k // NX, NY), step(x, lax.rem(k, NX), NX)

    partner = dev(z, y, x, other)

    barrier = pltpu.get_barrier_semaphore()
    pl.semaphore_signal(barrier, inc=1, device_id=partner, device_id_type=MESH)

    near_by = [
        dev(step(z, 1, NZ), y, x, c), dev(step(z, NZ - 1, NZ), y, x, c),
        dev(z, step(y, 1, NY), x, c), dev(z, step(y, NY - 1, NY), x, c),
        dev(z, y, step(x, 1, NX), c), dev(z, y, step(x, NX - 1, NX), c),
    ]
    for to in near_by:
        pl.semaphore_signal(barrier, inc=1, device_id=to, device_id_type=MESH)

    def tell(r):
        for to in near_by:
            pl.semaphore_signal(rounds.at[r], inc=1, device_id=to, device_id_type=MESH)

    def hear(r):
        pl.semaphore_wait(rounds.at[r], len(near_by))

    def columns(slab, core):
        return pl.ds(pl.multiple_of((slab * 2 + core) * width, width), width)

    def mine(slab):
        return pl.ds(pl.multiple_of(slab * width, width), width)

    my_rows = pl.ds(pl.multiple_of(c * rows, rows), rows)
    other_rows = pl.ds(pl.multiple_of(other * rows, rows), rows)

    w_local = pltpu.make_async_copy(w_hbm, wb.at[pl.ds(x * per, per)], in_sem.at[3])
    w_local.start()
    pairs = ((k_hbm, kb), (v_hbm, vb), (q_hbm, qb))
    for t, (src, dst) in enumerate(pairs):
        for slab in range(NX):
            pltpu.make_async_copy(src.at[:, columns(slab, c)], dst.at[my_rows, mine(slab)], in_sem.at[t]).start()

    pl.semaphore_wait(barrier, len(near_by) + 1)
    tell(0)

    right, left, far = step(x, 1, NX), step(x, NX - 1, NX), step(x, 2, NX)

    even = lax.rem(z, 2)
    up, down = step(z, 1, NZ), step(z, NZ - 1, NZ)
    order = (x, right, left, far)

    def feature_copy(src, g, target, sem):
        return pltpu.make_async_remote_copy(
            src_ref=src, dst_ref=wb.at[g], send_sem=sem, recv_sem=w_recv.at[g],
            device_id=target, device_id_type=MESH,
        )

    def feature_sends():
        for n in range(2):
            for direction, (target, b) in enumerate(((left, n), (right, 1 - n))):
                i = 2 * even + b
                yield feature_copy(w_hbm.at[i], x * per + i, dev(z, y, target, c), w_send.at[direction, b])


    def feature_up(slab, b):
        g = slab * per + 2 * even + b
        return feature_copy(wb.at[g], g, dev(up + (down - up) * b, y, x, c), wz_send.at[slab, b])

    def feature_on(slab, b, target):
        g = slab * per + 2 * even + b
        return feature_copy(wb.at[g], g, dev(z, y, target, c), wf_send.at[b])

    def feature_wait(g):
        feature_copy(wb.at[g], g, partner, w_send.at[0, 0]).wait_recv()

    def exchange(t, n):
        src, dst = pairs[t]
        slab = order[n]
        pltpu.make_async_remote_copy(
            src_ref=src.at[:, columns(slab, other)], dst_ref=dst.at[my_rows, mine(slab)],
            send_sem=ex_send.at[t], recv_sem=ex_recv.at[t, n], device_id=partner, device_id_type=MESH,
        ).start()

    def exchanged(t, n):
        view = pairs[t][1].at[other_rows, mine(order[n])]
        pltpu.make_async_remote_copy(
            src_ref=view, dst_ref=view, send_sem=ex_send.at[t], recv_sem=ex_recv.at[t, n],
            device_id=partner, device_id_type=MESH,
        ).wait_recv()

    for t in range(2):
        exchange(t, 0)
    for copy in feature_sends():
        copy.start()
    for n in range(1, NX):
        for t in range(2):
            exchange(t, n)
    for n in range(NX):
        exchange(2, n)
    w_local.wait()
    for t, (src, dst) in enumerate(pairs):
        pltpu.make_async_copy(dst.at[my_rows], dst.at[my_rows], in_sem.at[t]).wait()

    def owner(g):
        return dev(z, lax.rem(g, per), g // per, c)

    def s_copy(g, w):
        view = piece(w)
        return pltpu.make_async_remote_copy(
            src_ref=s_send.at[g, view], dst_ref=s_recv.at[p_me, view], send_sem=s_ssem,
            recv_sem=s_rsem.at[w, p_me], device_id=owner(g), device_id_type=MESH,
        )

    def t_copy(g):
        return pltpu.make_async_remote_copy(
            src_ref=t_send.at[g], dst_ref=t_recv.at[p_me], send_sem=t_ssem,
            recv_sem=t_rsem.at[p_me], device_id=owner(g), device_id_type=MESH,
        )

    at = lax.broadcasted_iota(jnp.int32, (tokens, tokens), 0)
    of = lax.broadcasted_iota(jnp.int32, (tokens, tokens), 1)
    causal = at >= of

    def mapped(source, dirs, dir_scale):
        wide = source.astype(F32)
        total = jnp.sum(wide * wide, axis=1, keepdims=True)
        r = lax.rsqrt(total * (1.0 / head_size) + 1e-06)
        halved = (0.5 * root * root * LOG2E) * total * r * r + 0.5 * math.log2(feats)
        return jnp.exp2(dot(source, dirs, (1, 1)) * (r * (root * LOG2E)) * dir_scale - halved)

    def head_columns(g):
        return pl.ds(pl.multiple_of(g * head_size, head_size), head_size)

    ones = jnp.ones((8, head_size), BF16)

    def key_parts(gs, early=EARLY):
        for g in gs:
            cols = head_columns(g)
            dirs = wb[g]
            square = dirs.astype(F32) * dirs.astype(F32)
            high = square.astype(BF16)
            low = (square - high.astype(F32)).astype(BF16)
            total = dot(ones, high, (1, 1)) + dot(ones, low, (1, 1))
            dir_scale = lax.rsqrt(total[0:1] * (1.0 / head_size) + 1e-06)
            scale[g] = dir_scale
            key_map = mapped(kb[:, cols], dirs, dir_scale).astype(BF16)
            phi_k[g] = key_map
            t_send[g] = jnp.sum(key_map.astype(F32), axis=0, keepdims=True)
            s_send[g] = dot(key_map, vb[:, cols], (0, 0)).astype(BF16)
        for g in gs:
            @pl.when(g != g_me)
            def _():
                t_copy(g).start()
                for w in range(early):
                    s_copy(g, w).start()

            @pl.when(g == g_me)
            def _():
                s_recv[p_me] = s_send[g]
                t_recv[p_me] = t_send[g]

    def query_parts(gs):
        for g in gs:
            cols = head_columns(g)
            query_map = mapped(qb[:, cols], wb[g], scale[g]).astype(BF16)
            phi_q[g] = query_map
            scores = jnp.where(causal, dot(query_map, phi_k[g], (1, 1)), 0.0)
            den[g] = jnp.sum(scores, axis=1, keepdims=True)
            num[g] = dot(scores.astype(BF16), vb[:, cols], (1, 0))

    def queries_of(n):
        exchanged(2, n)

        @pl.loop(0, per, step=2)
        def _(i):
            query_parts([order[n] * per + i, order[n] * per + i + 1])

    def near(n, own):
        side = n % 2
        b = (n // 2 + side) % 2
        slab = (right, left)[side]
        return slab, b, slab * per + 2 * (even if own else 1 - even) + b

    def pass_on(n):
        slab, b, g = near(n, True)
        feature_wait(g)
        if n < 2:
            feature_on(slab, b, (left, right)[n % 2]).start()
        feature_up(slab, b).start()

    def pass_far(b):
        feature_wait(far * per + 2 * even + b)
        feature_up(far, b).start()

    for t in range(2):
        exchanged(t, 0)
    hear(0)
    tell(1)
    key_parts([x * per, x * per + 1], WAVES)
    hear(1)
    tell(2)
    pass_on(0)
    pass_on(1)
    key_parts([x * per + 2, x * per + 3], WAVES)
    pass_on(2)
    pass_on(3)
    for n in (1, 2):
        for t in range(2):
            exchanged(t, n)
    hear(2)
    key_parts([near(0, True)[2], near(1, True)[2]])
    pass_far(0)
    key_parts([near(2, True)[2], near(3, True)[2]])
    pass_far(1)
    for t in range(2):
        exchanged(t, 3)
    key_parts([far * per + 2 * even, far * per + 2 * even + 1])
    late = [near(n, False)[2] for n in range(4)] + [far * per + 2 * (1 - even) + b for b in range(2)]
    for n in range(0, 6, 2):
        feature_wait(late[n])
        feature_wait(late[n + 1])
        key_parts(late[n:n + 2])

    for w in range(EARLY, WAVES):
        for dx in (1, 3, 2):
            @pl.loop(0, per)
            def _(dy):
                s_copy(step(x, dx, NX) * per + step(y, dy, NY), w).start()

    def z_copy(w, to):
        return pltpu.make_async_remote_copy(
            src_ref=z_send.at[piece(w)], dst_ref=z_recv.at[z, piece(w)], send_sem=z_ssem.at[w, to],
            recv_sem=z_rsem.at[w, z], device_id=dev(to, y, x, c), device_id_type=MESH,
        )

    def z_arrival(w, of_z):
        return pltpu.make_async_remote_copy(
            src_ref=z_send.at[piece(w)], dst_ref=z_recv.at[of_z, piece(w)], send_sem=z_ssem.at[w, of_z],
            recv_sem=z_rsem.at[w, of_z], device_id=dev(of_z, y, x, c), device_id_type=MESH,
        )

    def zt_copy(to, slot):
        return pltpu.make_async_remote_copy(
            src_ref=zt_send, dst_ref=zt_recv.at[slot], send_sem=zt_ssem.at[to],
            recv_sem=zt_rsem.at[slot], device_id=dev(to, y, x, c), device_id_type=MESH,
        )

    def gather(w):
        view = piece(w)

        @pl.loop(1, PLANE)
        def _(k):
            yy, xx = turned(k)
            p = yy * NX + xx
            pltpu.make_async_remote_copy(
                src_ref=s_send.at[0, view], dst_ref=s_recv.at[p, view], send_sem=s_ssem,
                recv_sem=s_rsem.at[w, p], device_id=dev(z, yy, xx, c), device_id_type=MESH,
            ).wait_recv()
            if w == 0:
                pltpu.make_async_remote_copy(
                    src_ref=t_send.at[0], dst_ref=t_recv.at[p], send_sem=t_ssem,
                    recv_sem=t_rsem.at[p], device_id=dev(z, yy, xx, c), device_id_type=MESH,
                ).wait_recv()

        total = s_recv[0, view].astype(F32)
        for p in range(1, PLANE):
            total = total + s_recv[p, view].astype(F32)
        z_send[piece(w)] = total.astype(BF16)
        if w == 0:
            sums = t_recv[0]
            for p in range(1, PLANE):
                sums = sums + t_recv[p]
            zt_send[...] = sums

        @pl.loop(z + 1, NZ)
        def _(to):
            z_copy(w, to).start()
            if w == 0:
                zt_copy(to, z).start()

    def p_copy(w, yy, xx):
        view = piece(w)
        p = yy * NX + xx
        return pltpu.make_async_remote_copy(
            src_ref=p_send.at[p, view], dst_ref=p_recv.at[g_me, view], send_sem=p_ssem,
            recv_sem=p_rsem.at[w, g_me], device_id=dev(z, yy, xx, c), device_id_type=MESH,
        )

    def pt_copy(yy, xx):
        p = yy * NX + xx
        return pltpu.make_async_remote_copy(
            src_ref=pt_send.at[p], dst_ref=pt_recv.at[g_me], send_sem=pt_ssem,
            recv_sem=pt_rsem.at[g_me], device_id=dev(z, yy, xx, c), device_id_type=MESH,
        )

    def spread(w):
        view = piece(w)

        def add(n, base):
            z_arrival(w, n).wait_recv()
            return base + z_recv[n, piece(w)].astype(F32)

        base = lax.fori_loop(0, z, add, jnp.zeros((starts[w + 1] - starts[w], head_size), F32))
        for p in range(PLANE):
            p_send[p, view] = base.astype(BF16)
            if p < PLANE - 1:
                base = base + s_recv[p, view].astype(F32)
        if w == 0:
            def add_totals(n, sums):
                zt_copy(n, n).wait_recv()
                return sums + zt_recv[n]

            sums = lax.fori_loop(0, z, add_totals, jnp.zeros((1, feats), F32))
            for p in range(PLANE):
                pt_send[p] = sums
                if p < PLANE - 1:
                    sums = sums + t_recv[p]
            pt_recv[g_me] = pt_send[p_me]
        p_recv[g_me, view] = p_send[p_me, view]

        @pl.loop(1, PLANE)
        def _(k):
            yy, xx = turned(k)
            p_copy(w, yy, xx).start()
            if w == 0:
                pt_copy(yy, xx).start()

    for stage in SCHEDULE:
        kind, n = stage[0], int(stage[1])
        if kind == "q":
            queries_of(n)
        elif kind == "g":
            gather(n)
        else:
            spread(n)

    def arrive(g):
        @pl.when(g != g_me)
        def _():
            for w in range(WAVES):
                view = piece(w)
                pltpu.make_async_remote_copy(
                    src_ref=p_send.at[0, view], dst_ref=p_recv.at[g, view], send_sem=p_ssem,
                    recv_sem=p_rsem.at[w, g], device_id=owner(g), device_id_type=MESH,
                ).wait_recv()

    def finish(g):
        ob[:, head_columns(g)] = ((num[g] + dot(phi_q[g], p_recv[g], (1, 0))) * den[g]).astype(BF16)

    def normalizer(g):
        @pl.when(g != g_me)
        def _():
            pltpu.make_async_remote_copy(
                src_ref=pt_send.at[0], dst_ref=pt_recv.at[g], send_sem=pt_ssem,
                recv_sem=pt_rsem.at[g], device_id=owner(g), device_id_type=MESH,
            ).wait_recv()

        den[g] = 1.0 / (den[g] + jnp.sum(phi_q[g].astype(F32) * pt_recv[g], axis=1, keepdims=True))

    def out_columns(g, core):
        at_head = (g // per * 2 + core) * per + lax.rem(g, per)
        return pl.ds(pl.multiple_of(at_head * head_size, head_size), head_size)

    def keep(g):
        cols = head_columns(g)
        return pltpu.make_async_copy(ob.at[my_rows, cols], out_hbm.at[:, out_columns(g, c)], o_sem.at[g])

    def give(g):
        cols = head_columns(g)
        return pltpu.make_async_remote_copy(
            src_ref=ob.at[other_rows, cols], dst_ref=out_hbm.at[:, out_columns(g, c)],
            send_sem=o_ssem.at[g], recv_sem=o_rsem.at[g], device_id=partner, device_id_type=MESH,
        )

    @pl.loop(0, heads)
    def _(k):
        normalizer(step(x * per, k, heads))

    @pl.loop(0, heads, step=2)
    def _(k):
        g = step(x * per, k, heads)
        arrive(g)
        arrive(g + 1)
        finish(g)
        finish(g + 1)
        for gg in (g, g + 1):
            give(gg).start()
            keep(gg).start()

    for copy in feature_sends():
        copy.wait_send()
    for b, slab in enumerate((right, left)):
        feature_on(slab, b, x).wait_send()
    for slab in (right, left, far):
        for b in range(2):
            feature_up(slab, b).wait_send()
    for t in range(3):
        view = pairs[t][1].at[other_rows]
        pltpu.make_async_remote_copy(
            src_ref=view, dst_ref=view, send_sem=ex_send.at[t], recv_sem=ex_recv.at[t, 0],
            device_id=partner, device_id_type=MESH,
        ).wait_send()

    def all_sent(src, dst, sem, recv_sem):
        pltpu.make_async_remote_copy(
            src_ref=src.at[pl.ds(0, PLANE - 1)], dst_ref=dst.at[pl.ds(0, PLANE - 1)], send_sem=sem,
            recv_sem=recv_sem, device_id=partner, device_id_type=MESH,
        ).wait_send()

    all_sent(s_send, s_recv, s_ssem, s_rsem.at[0, 0])
    all_sent(t_send, t_recv, t_ssem, t_rsem.at[0])
    all_sent(p_send, p_recv, p_ssem, p_rsem.at[0, 0])
    all_sent(pt_send, pt_recv, pt_ssem, pt_rsem.at[0])

    @pl.loop(z + 1, NZ)
    def _(to):
        for w in range(WAVES):
            z_copy(w, to).wait_send()
        zt_copy(to, z).wait_send()

    @pl.loop(0, heads)
    def _(g):
        keep(g).wait()
        give(g).wait_send()
        arrived = out_hbm.at[:, out_columns(g, other)]
        pltpu.make_async_remote_copy(
            src_ref=ob.at[other_rows, head_columns(g)], dst_ref=arrived,
            send_sem=o_ssem.at[g], recv_sem=o_rsem.at[g], device_id=partner, device_id_type=MESH,
        ).wait_recv()


def body(queries, keys, values, features):
    rows, width = queries.shape[1:]
    local_heads, feats, head_size = features.shape
    heads = local_heads * NX
    tokens = 2 * rows
    half = heads * head_size
    dma, vmem = pltpu.SemaphoreType.DMA, pltpu.VMEM
    any_space = pl.BlockSpec(memory_space=pl.ANY)
    state = (heads, feats, head_size)
    sums = (heads, 1, feats)
    out = pl.pallas_call(
        kernel,
        out_shape=jax.ShapeDtypeStruct((rows, width), BF16),
        in_specs=[any_space] * 4,
        out_specs=any_space,
        scratch_shapes=[
            vmem((tokens, half), BF16), vmem((tokens, half), BF16), vmem((tokens, half), BF16),
            vmem(state, BF16), vmem(sums, F32), vmem((heads, tokens, feats), BF16), vmem((heads, tokens, feats), BF16),
            vmem((heads, tokens, head_size), F32), vmem((heads, tokens, 1), F32), vmem((tokens, half), BF16),
            vmem(state, BF16), vmem(state, BF16), vmem(sums, F32), vmem(sums, F32),
            vmem((feats, head_size), BF16), vmem((NZ, feats, head_size), BF16),
            vmem((1, feats), F32), vmem((NZ, 1, feats), F32),
            vmem(state, BF16), vmem(state, BF16), vmem(sums, F32), vmem(sums, F32),
            dma((4,)), dma((3,)), dma((3, NX)), dma((2, 2)), dma((heads,)), dma((2,)), dma((NX, 2)),
            dma, dma((WAVES, PLANE)), dma, dma((PLANE,)), dma((WAVES, NZ)), dma((WAVES, NZ)), dma((NZ,)), dma((NZ,)),
            dma, dma((WAVES, heads)), dma, dma((heads,)), dma((heads,)), dma((heads,)), dma((heads,)),
            pltpu.SemaphoreType.REGULAR((3,)),
        ],
        compiler_params=pltpu.CompilerParams(
            collective_id=0, has_side_effects=True, vmem_limit_bytes=40 * 1024 * 1024
        ),
    )(*(pltpu.with_memory_space_constraint(a, pltpu.HBM) for a in (
        queries.reshape(rows, width), keys.reshape(rows, width), values.reshape(rows, width), features)))
    return out.reshape(1, rows, width)


def solution(mesh):
    tokens = P(None, ("seq", "head"), None)
    return jax.shard_map(
        body, mesh=mesh, in_specs=(tokens, tokens, tokens, P("head", None, None)), out_specs=tokens, check_vma=False
    )
```
